512 devices in a mesh: pos: 64 (over z, y_lo, x), head: 8 (over y_hi, core).
Axes of the slice: x: 4, y: 8 (y_hi: 4, y_lo: 2; y = y_hi * 2 + y_lo), z: 8, core: 2. Of those that a mesh axis runs over, the one named last changes fastest.
Arguments:
- token_ids: int32 [65536], P('pos'), may hold values from 0 to 255
- token_table: float32 [256, 1024], replicated, may hold values from -6 to 6
- row_table: float32 [256, 1024], replicated, may hold values from -6 to 6
- col_table: float32 [256, 1024], replicated, may hold values from -6 to 6
- chan_table: float32 [3, 1024], replicated, may hold values from -6 to 6
- w_query: float32 [1024, 1024], P(None, 'head'), as said below
- w_key: float32 [1024, 1024], P(None, 'head'), as said below
- w_value: float32 [1024, 1024], P(None, 'head'), may hold values from -0.1875 to 0.1875
- w_out: float32 [1024, 1024], P('head', 'pos'), may hold values from -0.1875 to 0.1875
- w_in: float32 [1024, 4096], P('pos', 'head'), may hold values from -0.1875 to 0.1875
- w_down: float32 [4096, 1024], P('head', 'pos'), may hold values from -0.09375 to 0.09375
Outputs:
- latent_out: float32 [512, 1024], P('pos')
The draws below stay inside these ranges and needn't reach their ends.
Inputs may be any that keep to these rules, and one draw needn't show every extreme that they name: `w_query`: entries of order 1024^-0.5 times a few. `w_key`: entries of order 1024^-0.5 times a few, or larger.
All inputs are finite; a program needn't handle non-finite values.
Results may differ from the reference program's by a relative error of at most 0.0003.
Values sent between devices are 32-bit elements; how exact they have to be, the bound alone decides.
No kernel may reach another device: no remote copies, remote signals or barrier semaphores. Data moves between devices by JAX's collectives and lax.ppermute only.
A program may use at most 128 MiB of HBM per device.

```python
import jax
import jax.numpy as jnp
from jax import lax

D = 1024
HEADS = 16
HD = 64
FF = 4096
VOCAB = 256
IMG = 256
LAT = 512
POS_DEV = 1024
POSITIONS = 65536


def query_key_pair(key):
    first = jnp.clip(jax.random.normal(jax.random.fold_in(key, 11), (D, HEADS * HD), jnp.float32), -6.0, 6.0) * D ** (-0.5)
    second = jnp.clip(jax.random.normal(jax.random.fold_in(key, 12), (D, HEADS * HD), jnp.float32), -6.0, 6.0) * D ** (-0.5)
    return (first, second)


def draw_w_query(key, part):
    first, second = query_key_pair(key)
    return first


def draw_w_key(key, part):
    first, second = query_key_pair(key)
    return second


def place_ends(result, rng, least, largest):
    longest = result.shape.index(max(result.shape))
    spots = []
    for shift in (0, 1):
        where = [jax.random.randint(jax.random.fold_in(rng, axis), (), 0, length) for axis, length in enumerate(result.shape)]
        where[longest] = (where[longest] + shift) % result.shape[longest]
        spots.append(tuple(where))
    return result.at[spots[0]].set(least).at[spots[1]].set(largest)


def levels(own_key, dims, split, smallest, high):
    def one(axis_at, blocks):
        steps = jax.random.uniform(jax.random.fold_in(jax.random.fold_in(own_key, 6), axis_at), (blocks,), jnp.float32, smallest / len(split), high / len(split))
        return jnp.repeat(jnp.exp(steps), dims[axis_at] // blocks).reshape((-1,) + (1,) * (len(dims) - axis_at - 1))

    loudness = one(*split[0])
    for cut in split[1:]:
        loudness = loudness * one(*cut)
    return loudness


def bell_draw(own_key, shape, deviation, most, shards=(), kind=jnp.bfloat16):
    values = deviation * jax.random.normal(own_key, shape, jnp.float32)
    if shards:
        values = values * levels(own_key, shape, shards, -0.22, 0.18)
    return jnp.clip(values, -most, most).astype(kind)


def setup_inputs(seed: int = 0) -> dict:
    splits = jax.random.split(jax.random.key(seed), 12)
    token_ids = place_ends(jax.random.randint(splits[0], (POSITIONS,), 0, VOCAB), jax.random.fold_in(splits[0], 1), 0, VOCAB - 1).astype(jnp.int32)
    token_table = bell_draw(splits[1], (VOCAB, D), 1.0, 6.0, (), jnp.float32)
    row_table = bell_draw(splits[2], (IMG, D), 1.0, 6.0, (), jnp.float32)
    col_table = bell_draw(splits[3], (IMG, D), 1.0, 6.0, (), jnp.float32)
    chan_table = bell_draw(splits[4], (3, D), 1.0, 6.0, (), jnp.float32)
    w_query = draw_w_query(jax.random.fold_in(splits[11], 71), 0)
    w_key = draw_w_key(jax.random.fold_in(splits[11], 71), 0)
    w_value = bell_draw(splits[7], (D, HEADS * HD), D ** -0.5, 0.1875, ((1, 8),), jnp.float32)
    w_out = bell_draw(splits[8], (HEADS * HD, D), (HEADS * HD) ** -0.5, 0.1875, ((0, 8), (1, 64)), jnp.float32)
    w_in = bell_draw(splits[9], (D, FF), D ** -0.5, 0.1875, ((0, 64), (1, 8)), jnp.float32)
    w_down = bell_draw(splits[10], (FF, D), FF ** -0.5, 0.09375, ((0, 8), (1, 64)), jnp.float32)
    return {"token_ids": token_ids, "token_table": token_table, "row_table": row_table, "col_table": col_table, "chan_table": chan_table, "w_query": w_query, "w_key": w_key, "w_value": w_value, "w_out": w_out, "w_in": w_in, "w_down": w_down}


def layer_norm(values):
    center = values - lax.optimization_barrier(jnp.mean(values, axis=-1, keepdims=True))
    spread = lax.optimization_barrier(jnp.mean(center * center, axis=-1, keepdims=True))
    return center * lax.rsqrt(spread + 1e-05)

def embed(ids, where, token_table, row_table, col_table, chan_table):
    channel = where % 3
    pixel = where // 3
    image_row = pixel // IMG
    image_col = pixel % IMG
    summed = jnp.take(token_table, ids, axis=0) + jnp.take(row_table, image_row, axis=0)
    summed = summed + jnp.take(col_table, image_col, axis=0) + jnp.take(chan_table, channel, axis=0)
    return layer_norm(summed)

def reference(token_ids, token_table, row_table, col_table, chan_table, w_query, w_key, w_value, w_out, w_in, w_down):
    highest = lax.Precision.HIGHEST
    total = token_ids.shape[0]
    key_block = min(512, POS_DEV)
    lat_pos = (total - LAT + jnp.arange(LAT)).astype(jnp.int32)
    lat_emb = embed(token_ids[total - LAT:], lat_pos, token_table, row_table, col_table, chan_table)
    queries = jnp.dot(lat_emb, w_query, precision=highest).reshape(LAT, HEADS, HD).transpose(1, 0, 2) * HD ** (-0.5)

    def step(carry, start):
        top, weight, accum = carry
        where = (start + jnp.arange(key_block)).astype(jnp.int32)
        ids = lax.dynamic_slice_in_dim(token_ids, start, key_block)
        emb = embed(ids, where, token_table, row_table, col_table, chan_table)
        keys = jnp.dot(emb, w_key, precision=highest).reshape(key_block, HEADS, HD)
        vals = jnp.dot(emb, w_value, precision=highest).reshape(key_block, HEADS, HD)
        scores = jnp.einsum('hld,khd->hlk', queries, keys, precision=highest)
        scores = jnp.where(where[None, None, :] <= lat_pos[None, :, None], scores, -1e+30)
        new_top = jnp.maximum(top, lax.optimization_barrier(jnp.max(scores, axis=-1)))
        factor = jnp.exp(top - new_top)
        probs = jnp.exp(scores - new_top[..., None])
        weight = weight * factor + lax.optimization_barrier(jnp.sum(probs, axis=-1))
        accum = accum * factor[..., None] + jnp.einsum('hlk,khd->hld', probs, vals, precision=highest)
        return ((new_top, weight, accum), None)
    starts = (jnp.arange(total // key_block) * key_block).astype(jnp.int32)
    init = (jnp.full((HEADS, LAT), -1e+30, jnp.float32), jnp.zeros((HEADS, LAT), jnp.float32), jnp.zeros((HEADS, LAT, HD), jnp.float32))
    (top, weight, accum), _ = lax.scan(step, init, starts)
    attended = (accum / weight[..., None]).transpose(1, 0, 2).reshape(LAT, HEADS * HD)
    projected = jnp.dot(attended, w_out, precision=highest)
    hidden = jax.nn.gelu(jnp.dot(layer_norm(projected), w_in, precision=highest))
    return projected + jnp.dot(hidden, w_down, precision=highest)
```

```python
import functools

import jax
import jax.numpy as jnp
import numpy as np
from jax import lax
from jax.experimental import pallas as pl
from jax.experimental.pallas import tpu as pltpu
from jax.sharding import Mesh
from jax.sharding import PartitionSpec as P

D = 1024
HD = 64
IMG = 256
LAT = 512
POS_DEV = 1024
POSITIONS = 65536
VOCAB = 256
COL_AT = VOCAB
ROW_AT = COL_AT + IMG
ROWS_USED = 88
CHAN_AT = ROW_AT + ROWS_USED
STACK = 640

POS = ("z", "ylo", "x")
HEAD = ("yhi", "core")
PLANE = ("ylo", "x", "yhi", "core")

HIGHEST = lax.Precision.HIGHEST
NT = (((1,), (1,)), ((), ()))
NN = (((1,), (0,)), ((), ()))


def split_tables(token, row, col, chan, parts):
    def put(at, values):
        size = values.shape[0]
        for part in parts:
            rounded = values.astype(jnp.bfloat16)
            part[pl.ds(at, size), :] = rounded
            values = values - rounded.astype(jnp.float32)

    for block in range(2):
        put(block * 128, token[pl.ds(block * 128, 128), :])
        put(COL_AT + block * 128, col[pl.ds(block * 128, 128), :])
    tail = jnp.concatenate(
        [row[pl.ds(0, ROWS_USED), :], chan[...], jnp.zeros((128 - ROWS_USED - 3, D), jnp.float32)],
        axis=0,
    )
    put(ROW_AT, tail)


def embed(ids, first, parts):
    rows = ids.shape[0]
    base = first // 3
    step = lax.broadcasted_iota(jnp.int32, (rows, 1), 0) + (first - base * 3)
    third = (step * 21846) >> 16
    channel = step - third * 3
    pixel = base + third
    lane = lax.broadcasted_iota(jnp.int32, (rows, 256), 1)
    lane_tail = lax.broadcasted_iota(jnp.int32, (rows, 128), 1)

    def hot(mask):
        return jnp.where(mask, 1.0, 0.0).astype(jnp.bfloat16)

    tail = (lane_tail == (pixel >> 8)) | (lane_tail == channel + ROWS_USED)
    picks = jnp.concatenate([hot(lane == ids), hot(lane == (pixel & 255)), hot(tail)], axis=1)
    total = None
    for part in reversed(parts):
        piece = lax.dot_general(picks, part[...], NN, preferred_element_type=jnp.float32)
        total = piece if total is None else total + piece
    center = total - jnp.mean(total, axis=-1, keepdims=True)
    spread = jnp.mean(center * center, axis=-1, keepdims=True)
    return center * lax.rsqrt(spread + 1e-05)


def keys_kernel(index, ids, token, row, col, chan, w_key, w_value, keys, values, *parts):
    block = pl.program_id(0)

    @pl.when(block == 0)
    def _():
        split_tables(token, row, col, chan, parts)

    size = ids.shape[0]
    emb = embed(ids[...], index[0] * POS_DEV + block * size, parts)
    keys[...] = jnp.dot(emb, w_key[...], precision=HIGHEST)
    values[...] = jnp.dot(emb, w_value[...], precision=HIGHEST)


def attend_kernel(index, ids, token, row, col, chan, w_query, keys, values, out, *parts):
    block = pl.program_id(0)

    @pl.when(block == 0)
    def _():
        split_tables(token, row, col, chan, parts)

    size = ids.shape[0]
    first = POSITIONS - LAT + block * size
    emb = embed(ids[...], first, parts)
    queries = jnp.dot(emb, w_query[...], precision=HIGHEST) * HD ** (-0.5)
    low = lax.broadcasted_iota(jnp.int32, (size, 2 * HD), 1) < HD
    low_keys = lax.broadcasted_iota(jnp.int32, (POS_DEV, 2 * HD), 1) < HD
    where = index[0] * POS_DEV + lax.broadcasted_iota(jnp.int32, (size, POS_DEV), 1)
    latent = first + lax.broadcasted_iota(jnp.int32, (size, POS_DEV), 0)
    seen = where <= latent
    tops, weights, accum = [], [], None
    for head in range(2):
        own = low if head == 0 else ~low
        own_values = low_keys if head == 0 else ~low_keys
        scores = lax.dot_general(
            jnp.where(own, queries, 0.0), keys[...], NT, precision=HIGHEST,
            preferred_element_type=jnp.float32,
        )
        scores = jnp.where(seen, scores, -1e30)
        top = jnp.max(scores, axis=-1, keepdims=True)
        probs = jnp.exp(scores - top)
        tops.append(top)
        weights.append(jnp.sum(probs, axis=-1, keepdims=True))
        part = jnp.dot(probs, jnp.where(own_values, values[...], 0.0), precision=HIGHEST)
        accum = part if accum is None else accum + part
    weight = jnp.where(low, weights[0], weights[1])
    top = jnp.where(low, tops[0], tops[1])
    out[:, 0:8, :] = (accum / weight).reshape(size // 8, 8, 2 * HD)
    out[:, 8:16, :] = (top + jnp.log(weight)).reshape(size // 8, 8, 2 * HD)


def project_kernel(states, weights, out):
    level = states[:, 8:16, :]
    share = jnp.exp(level - jnp.max(level, axis=0, keepdims=True))
    attended = jnp.sum(share * states[:, 0:8, :], axis=0) / jnp.sum(share, axis=0)
    for c in range(8):
        block = weights[c * 8 : (c + 1) * 8, 0:16, :].reshape(128, 128)
        out[pl.ds(c, 8, stride=8), :] = lax.dot_general(
            attended, block, NT, precision=HIGHEST, preferred_element_type=jnp.float32
        )


def latent_kernel(rows, weights, out):
    pieces = [rows[pl.ds(c, 64, stride=8), :] for c in range(8)]
    mean = sum(jnp.sum(p, axis=-1, keepdims=True) for p in pieces) * (1.0 / D)
    pieces = [p - mean for p in pieces]
    spread = sum(jnp.sum(p * p, axis=-1, keepdims=True) for p in pieces) * (1.0 / D)
    scale = lax.rsqrt(spread + 1e-05)
    hidden = None
    blocks = []
    for c in range(8):
        block = weights[c * 8 : (c + 1) * 8, 16:32, :].reshape(128, 128)
        blocks.append(block)
        part = jnp.dot(pieces[c] * scale, block, precision=HIGHEST)
        hidden = part if hidden is None else hidden + part
    hidden = jax.nn.gelu(pltpu.roll(hidden, 64, 1))
    lane = lax.broadcasted_iota(jnp.int32, hidden.shape, 1)
    hidden = jnp.where(lane >= 64, hidden, 0.0)
    for c in range(8):
        out[pl.ds(c, 64, stride=8), :] = lax.dot_general(
            hidden, blocks[c], NT, precision=HIGHEST, preferred_element_type=jnp.float32
        )


VMEM = pl.BlockSpec(memory_space=pltpu.VMEM)
SMEM = pl.BlockSpec(memory_space=pltpu.SMEM)


def shape(*dims):
    return jax.ShapeDtypeStruct(dims, jnp.float32)


def params(**more):
    return pltpu.CompilerParams(vmem_limit_bytes=56 * 1024 * 1024, **more)


def exchange(value, axes):
    return lax.all_to_all(value, axes, 0, 0)


def per_device(token_ids, token_table, row_table, col_table, chan_table, w_query, w_key, w_value, w_out, w_in, w_down):
    index = lax.axis_index(POS).astype(jnp.int32).reshape(1)
    tables = (token_table, row_table, col_table, chan_table)

    with jax.named_scope("ids"):
        sent = jnp.broadcast_to(token_ids[POS_DEV - LAT :].reshape(1, 4, 128), (64, 4, 128))
        latent_ids = exchange(sent, POS)[63].reshape(LAT, 1)

    with jax.named_scope("weights"):
        own_out = jnp.broadcast_to(w_out.T.reshape(1, 16, 128), (8, 16, 128))
        own_in = w_in.reshape(16, 8, 64).transpose(1, 0, 2)
        own_down = w_down.reshape(8, 64, 16).transpose(0, 2, 1)
        packed = jnp.concatenate([own_out, jnp.concatenate([own_in, own_down], axis=2)], axis=1)
        packed = jnp.broadcast_to(packed[None], (8, 8, 32, 128)).reshape(64, 32, 128)
        packed, latent_ids = lax.optimization_barrier((packed, latent_ids))
        weights = exchange(packed, POS)

    block = 256
    whole = lambda i: (0, 0)
    table_specs = [
        pl.BlockSpec((VOCAB, D), whole),
        pl.BlockSpec((IMG, D), whole),
        pl.BlockSpec((IMG, D), whole),
        pl.BlockSpec((3, D), whole),
    ]
    splits = [pltpu.VMEM((STACK, D), jnp.bfloat16)] * 3
    keys, values = pl.pallas_call(
        keys_kernel,
        grid=(POS_DEV // block,),
        in_specs=[SMEM, pl.BlockSpec((block, 1), lambda i: (i, 0)), *table_specs]
        + [pl.BlockSpec((D, 128), whole)] * 2,
        out_specs=[pl.BlockSpec((block, 128), lambda i: (i, 0))] * 2,
        out_shape=[shape(POS_DEV, 128)] * 2,
        scratch_shapes=splits,
        compiler_params=params(),
        cost_estimate=pl.CostEstimate(flops=8 * 10**9, transcendentals=0, bytes_accessed=6 * 10**6),
        name="keys",
    )(index, token_ids.reshape(POS_DEV, 1), *tables, w_key, w_value)

    size = 128
    states = pl.pallas_call(
        attend_kernel,
        grid=(LAT // size,),
        in_specs=[SMEM, pl.BlockSpec((size, 1), lambda i: (i, 0)), *table_specs]
        + [pl.BlockSpec((D, 128), whole)]
        + [pl.BlockSpec((POS_DEV, 128), whole)] * 2,
        out_specs=pl.BlockSpec((size // 8, 16, 128), lambda i: (i, 0, 0)),
        out_shape=shape(64, 16, 128),
        scratch_shapes=splits,
        compiler_params=params(),
        cost_estimate=pl.CostEstimate(flops=10 * 10**9, transcendentals=10**6, bytes_accessed=6 * 10**6),
        name="attend",
    )(index, latent_ids, *tables, w_query, keys, values)

    with jax.named_scope("states"):
        states, weights = lax.optimization_barrier((states, weights))
        states = exchange(states, POS)
    partial_rows = pl.pallas_call(
        project_kernel,
        in_specs=[VMEM, VMEM],
        out_specs=VMEM,
        out_shape=shape(64, 128),
        compiler_params=params(),
        name="project",
    )(states, weights)
    with jax.named_scope("projected"):
        projected = jnp.sum(exchange(partial_rows.reshape(8, 8, 128), HEAD), axis=0)
        rows = exchange(jnp.broadcast_to(projected[None], (64, 8, 128)), PLANE)
    outs = pl.pallas_call(
        latent_kernel,
        in_specs=[VMEM, VMEM],
        out_specs=VMEM,
        out_shape=shape(512, 128),
        compiler_params=params(),
        name="latent",
    )(rows.reshape(512, 128), weights)
    with jax.named_scope("result"):
        own = projected + jnp.sum(exchange(outs.reshape(64, 8, 128), PLANE), axis=0)
        return exchange(jnp.broadcast_to(own[None], (8, 8, 128)), HEAD).reshape(8, D)


def solution(mesh):
    fine = Mesh(mesh.devices.reshape(8, 2, 4, 4, 2), ("z", "ylo", "x", "yhi", "core"))
    placed = (
        P(POS),
        P(),
        P(),
        P(),
        P(),
        P(None, HEAD),
        P(None, HEAD),
        P(None, HEAD),
        P(HEAD, POS),
        P(POS, HEAD),
        P(HEAD, POS),
    )
    return jax.shard_map(
        per_device, mesh=fine, in_specs=placed, out_specs=P(POS, None), check_vma=False
    )
```

```python
import jax
import jax.numpy as jnp
from jax import lax
from jax.experimental import pallas as pl
from jax.experimental.pallas import tpu as pltpu
from jax.sharding import Mesh
from jax.sharding import PartitionSpec as P

D = 1024
HD = 64
IMG = 256
LAT = 512
POS_DEV = 1024
POSITIONS = 65536
VOCAB = 256
ROWS_USED = 88

POS = ("z", "ylo", "x")
HEAD = ("yhi", "core")
COLUMN = ("ylo", "x")
SHARERS = ("z", "yhi", "core")

HIGHEST = lax.Precision.HIGHEST
NT = (((1,), (1,)), ((), ()))
NN = (((1,), (0,)), ((), ()))


def parts_of(values):
    parts = []
    for _ in range(3):
        rounded = values.astype(jnp.bfloat16)
        parts.append(rounded)
        values = values - rounded.astype(jnp.float32)
    return parts


def store_parts(refs, at, values):
    for ref, part in zip(refs, parts_of(values)):
        ref[pl.ds(at, values.shape[0]), :] = part


def place(first, rows):
    base = first // 3
    step = lax.broadcasted_iota(jnp.int32, (rows, 1), 0) + (first - base * 3)
    third = (step * 21846) >> 16
    return step - third * 3, base + third


def hot(mask):
    return jnp.where(mask, 1.0, 0.0).astype(jnp.bfloat16)


def hot_place(first, rows):
    channel, pixel = place(first, rows)
    lane = lax.broadcasted_iota(jnp.int32, (rows, 256), 1)
    tail = lax.broadcasted_iota(jnp.int32, (rows, 128), 1)
    in_tail = (tail == (pixel >> 8)) | (tail == channel + ROWS_USED)
    return jnp.concatenate([hot(lane == (pixel & 255)), hot(in_tail)], axis=1)


def hot_token(ids):
    return hot(lax.broadcasted_iota(jnp.int32, (ids.shape[0], VOCAB), 1) == ids)


def pick(picks, parts):
    total = None
    for part in reversed(parts):
        piece = lax.dot_general(picks, part, NN, preferred_element_type=jnp.float32)
        total = piece if total is None else total + piece
    return total


def normalized(total):
    center = total - jnp.mean(total, axis=-1, keepdims=True)
    spread = jnp.mean(center * center, axis=-1, keepdims=True)
    return center * lax.rsqrt(spread + 1e-05)


def low_lanes(rows):
    return lax.broadcasted_iota(jnp.int32, (rows, 2 * HD), 1) < HD


def pair(low, first, second, head):
    if head == 0:
        return jnp.where(low, first, pltpu.roll(second, HD, 1))
    return jnp.where(low, pltpu.roll(first, HD, 1), second)


def keys_kernel(index, ids, token, row, col, chan, w_key, w_value, key_cat, value_cat, where_sum, t1, t2, t3, p1, p2, p3):
    block = pl.program_id(0)
    tokens, places = (t1, t2, t3), (p1, p2, p3)

    @pl.when(block == 0)
    def _():
        for at in (0, 128):
            store_parts(tokens, at, token[pl.ds(at, 128), :])
            store_parts(places, at, col[pl.ds(at, 128), :])
        rest = jnp.zeros((128 - ROWS_USED - 3, D), jnp.float32)
        store_parts(places, 256, jnp.concatenate([row[pl.ds(0, ROWS_USED), :], chan[...], rest], axis=0))

    size = ids.shape[0]
    lat_size = where_sum.shape[0]
    where_parts = [p[...] for p in places]
    first = index[0] * POS_DEV + block * size
    total = pick(hot_place(first, size), where_parts) + pick(hot_token(ids[...]), [t[...] for t in tokens])
    emb = normalized(total)
    keys = jnp.dot(emb, w_key[...], precision=HIGHEST)
    values = jnp.dot(emb, w_value[...], precision=HIGHEST)
    low = low_lanes(size)
    k = [part.astype(jnp.float32) for part in parts_of(keys)]
    v = [part.astype(jnp.float32) for part in parts_of(values)]
    ones = jnp.ones_like(values)
    for head in range(2):
        both = pair(low, k[0], k[1], head)
        pieces = [both, both, pair(low, k[2], k[0], head), pair(low, k[2], k[1], head)]
        for i, piece in enumerate(pieces):
            key_cat[head, :, i * 128 : (i + 1) * 128] = piece.astype(jnp.bfloat16)
        tail = jnp.where(low, v[2], ones) if head == 0 else jnp.where(low, ones, v[2])
        value_cat[head, :, 0:128] = pair(low, v[0], v[1], head).astype(jnp.bfloat16)
        value_cat[head, :, 128:256] = tail.astype(jnp.bfloat16)
    where_sum[...] = pick(hot_place(POSITIONS - LAT + block * lat_size, lat_size), where_parts)


def attend_kernel(index, ids, where_sum, t1, t2, t3, w_query, key_cat, value_cat, out, attended):
    block = pl.program_id(0)
    size = ids.shape[0]
    emb = normalized(where_sum[...] + pick(hot_token(ids[...]), [t1[...], t2[...], t3[...]]))
    queries = jnp.dot(emb, w_query[...], precision=HIGHEST) * HD ** (-0.5)
    q = [part.astype(jnp.float32) for part in parts_of(queries)]
    low = low_lanes(size)
    where = index[0] * POS_DEV + lax.broadcasted_iota(jnp.int32, (size, POS_DEV), 1)
    latent = POSITIONS - LAT + block * size + lax.broadcasted_iota(jnp.int32, (size, POS_DEV), 0)
    seen = where <= latent
    sums, weights, tops = [], [], []
    for head in range(2):
        query_cat = jnp.concatenate(
            [pair(low, q[0], q[0], head), pair(low, q[1], q[1], head)]
            + [pair(low, q[0], q[2], head), pair(low, q[1], q[2], head)],
            axis=1,
        ).astype(jnp.bfloat16)
        scores = lax.dot_general(query_cat, key_cat[head], NT, preferred_element_type=jnp.float32)
        scores = jnp.where(seen, scores, -1e30)
        top = jnp.max(scores, axis=-1, keepdims=True)
        probs = jnp.exp(scores - top)
        near = probs.astype(jnp.bfloat16)
        rest = (probs - near.astype(jnp.float32)).astype(jnp.bfloat16)
        value = value_cat[head]
        both = jnp.dot(near, value, preferred_element_type=jnp.float32)
        both = both + jnp.dot(rest, value, preferred_element_type=jnp.float32)
        lead, tail = both[:, :128], both[:, 128:]
        sums.append(lead + pltpu.roll(lead, HD, 1) + tail)
        weights.append(pltpu.roll(tail, HD, 1))
        tops.append(top)
    weight = jnp.where(low, weights[0], weights[1])
    level = jnp.where(low, tops[0], tops[1]) + jnp.log(weight)
    attended[...] = jnp.where(low, sums[0], sums[1]) / weight
    chunks = size // 8
    for r in range(8):
        out[pl.ds(r, chunks, stride=9), :] = attended[pl.ds(r, chunks, stride=8), :]
    level = level.reshape(chunks, 8, 128)
    lane = lax.broadcasted_iota(jnp.int32, level.shape, 2)
    lat = lax.broadcasted_iota(jnp.int32, level.shape, 1)
    out[pl.ds(8, chunks, stride=9), :] = jnp.sum(jnp.where((lane & 7) == lat, level, 0.0), axis=1)


def project_kernel(states, weights, out):
    levels = states[pl.ds(8, 64, stride=9), :]
    low = low_lanes(64)
    rows = []
    for r in range(8):
        level = jnp.where(low, levels[:, r : r + 1], levels[:, HD + r : HD + r + 1])
        share = jnp.exp(level - jnp.max(level, axis=0, keepdims=True))
        value = jnp.sum(share * states[pl.ds(r, 64, stride=9), :], axis=0, keepdims=True)
        rows.append(value / jnp.sum(share, axis=0, keepdims=True))
    attended = jnp.concatenate(rows, axis=0)
    for c in range(8):
        block = weights[:, c * 32 : c * 32 + 16, :].reshape(128, 128)
        out[pl.ds(c, 8, stride=8), :] = lax.dot_general(
            attended, block, NT, precision=HIGHEST, preferred_element_type=jnp.float32
        )


def latent_kernel(rows, weights, out):
    pieces = [rows[pl.ds(c, 64, stride=8), :] for c in range(8)]
    mean = sum(jnp.sum(p, axis=-1, keepdims=True) for p in pieces) * (1.0 / D)
    pieces = [p - mean for p in pieces]
    spread = sum(jnp.sum(p * p, axis=-1, keepdims=True) for p in pieces) * (1.0 / D)
    scale = lax.rsqrt(spread + 1e-05)
    hidden = None
    blocks = []
    for c in range(8):
        block = weights[:, c * 32 + 16 : c * 32 + 32, :].reshape(128, 128)
        blocks.append(block)
        part = jnp.dot(pieces[c] * scale, block, precision=HIGHEST)
        hidden = part if hidden is None else hidden + part
    hidden = jax.nn.gelu(pltpu.roll(hidden, 64, 1))
    lane = lax.broadcasted_iota(jnp.int32, hidden.shape, 1)
    hidden = jnp.where(lane >= 64, hidden, 0.0)
    for c in range(8):
        out[pl.ds(c, 64, stride=8), :] = lax.dot_general(
            hidden, blocks[c], NT, precision=HIGHEST, preferred_element_type=jnp.float32
        )


VMEM = pl.BlockSpec(memory_space=pltpu.VMEM)
SMEM = pl.BlockSpec(memory_space=pltpu.SMEM)


def shape(*dims):
    return jax.ShapeDtypeStruct(dims, jnp.float32)


def params(**more):
    return pltpu.CompilerParams(vmem_limit_bytes=56 * 1024 * 1024, **more)


def exchange(value, axes):
    return lax.all_to_all(value, axes, 0, 0)


def per_device(token_ids, token_table, row_table, col_table, chan_table, w_query, w_key, w_value, w_out, w_in, w_down):
    index = lax.axis_index(POS).astype(jnp.int32).reshape(1)

    with jax.named_scope("weights"):
        own_ids = token_ids[POS_DEV - LAT :].astype(jnp.float32).reshape(4, 128)
        own_ids = jnp.concatenate([own_ids, jnp.zeros((4, 128), jnp.float32)], axis=0)
        own_in = w_in.reshape(16, 8, 64).transpose(1, 0, 2)
        own_down = w_down.reshape(8, 64, 16).transpose(0, 2, 1)
        packed = jnp.concatenate(
            [
                jnp.broadcast_to(w_out.T[None], (8, 16, 128)),
                jnp.concatenate([own_in, own_down], axis=2),
                jnp.broadcast_to(own_ids[None], (8, 8, 128)),
            ],
            axis=1,
        )
        packed = exchange(packed, "z")
        packed = jnp.concatenate([packed[:, :32, :].reshape(256, 128), packed[7, 32:, :]], axis=0)
        weights = exchange(jnp.broadcast_to(packed[None], (8, 264, 128)), COLUMN)
        latent_ids = weights[7, 256:260, :].astype(jnp.int32).reshape(LAT, 1)

    steps = 4
    block, size = POS_DEV // steps, LAT // steps
    bf16 = lambda *dims: jax.ShapeDtypeStruct(dims, jnp.bfloat16)
    whole = lambda *dims: pl.BlockSpec(dims, lambda i: (0,) * len(dims))
    slab = lambda *dims: pl.BlockSpec(dims, lambda i: (i,) + (0,) * (len(dims) - 1))
    middle = lambda *dims: pl.BlockSpec(dims, lambda i: (0, i, 0))
    key_cat, value_cat, where_sum, *tokens = pl.pallas_call(
        keys_kernel,
        grid=(steps,),
        in_specs=[SMEM, slab(block, 1), whole(VOCAB, D), whole(IMG, D), whole(IMG, D), whole(3, D)]
        + [whole(D, 128)] * 2,
        out_specs=[middle(2, block, 512), middle(2, block, 256), slab(size, D)] + [whole(VOCAB, D)] * 3,
        out_shape=[bf16(2, POS_DEV, 512), bf16(2, POS_DEV, 256), shape(LAT, D)] + [bf16(VOCAB, D)] * 3,
        scratch_shapes=[pltpu.VMEM((384, D), jnp.bfloat16)] * 3,
        compiler_params=params(),
        cost_estimate=pl.CostEstimate(flops=8 * 10**9, transcendentals=0, bytes_accessed=10**7),
        name="keys",
    )(index, token_ids.reshape(POS_DEV, 1), token_table, row_table, col_table, chan_table, w_key, w_value)

    states = pl.pallas_call(
        attend_kernel,
        grid=(steps,),
        in_specs=[SMEM, slab(size, 1), slab(size, D)]
        + [whole(VOCAB, D)] * 3
        + [whole(D, 128), whole(2, POS_DEV, 512), whole(2, POS_DEV, 256)],
        out_specs=slab(size // 8 * 9, 128),
        out_shape=shape(64 * 9, 128),
        scratch_shapes=[pltpu.VMEM((size, 128), jnp.float32)],
        compiler_params=params(),
        cost_estimate=pl.CostEstimate(flops=6 * 10**9, transcendentals=10**6, bytes_accessed=10**7),
        name="attend",
    )(index, latent_ids, where_sum, *tokens, w_query, key_cat, value_cat)

    with jax.named_scope("states"):
        states = exchange(states.reshape(64, 1, 1152), POS).reshape(64 * 9, 128)
    partial_rows = pl.pallas_call(
        project_kernel,
        in_specs=[VMEM, VMEM],
        out_specs=VMEM,
        out_shape=shape(64, 128),
        compiler_params=params(),
        name="project",
    )(states, weights)
    with jax.named_scope("projected"):
        projected = jnp.sum(exchange(partial_rows.reshape(8, 8, 128), HEAD), axis=0)
        rows = exchange(jnp.broadcast_to(projected[None], (64, 8, 128)), SHARERS)
    outs = pl.pallas_call(
        latent_kernel,
        in_specs=[VMEM, VMEM],
        out_specs=VMEM,
        out_shape=shape(512, 128),
        compiler_params=params(),
        name="latent",
    )(rows.reshape(512, 128), weights)
    with jax.named_scope("result"):
        own = projected + jnp.sum(exchange(outs.reshape(64, 8, 128), SHARERS), axis=0)
        return exchange(jnp.broadcast_to(own[None], (8, 8, 128)), HEAD).reshape(8, D)


def solution(mesh):
    fine = Mesh(mesh.devices.reshape(8, 2, 4, 4, 2), ("z", "ylo", "x", "yhi", "core"))
    placed = (
        P(POS),
        P(),
        P(),
        P(),
        P(),
        P(None, HEAD),
        P(None, HEAD),
        P(None, HEAD),
        P(HEAD, POS),
        P(POS, HEAD),
        P(HEAD, POS),
    )
    return jax.shard_map(
        per_device, mesh=fine, in_specs=placed, out_specs=P(POS, None), check_vma=False
    )
```

```python
import jax
import jax.numpy as jnp
from jax import lax
from jax.experimental import pallas as pl
from jax.experimental.pallas import tpu as pltpu
from jax.sharding import Mesh
from jax.sharding import PartitionSpec as P

D = 1024
HD = 64
IMG = 256
LAT = 512
POS_DEV = 1024
POSITIONS = 65536
VOCAB = 256
ROWS_USED = 88
KEY_STEPS = 2
LATENT_STEPS = 2

POS = ("z", "ylo", "x")
HEAD = ("yhi", "core")
COLUMN = ("ylo", "x")
SHARERS = ("z", "yhi", "core")

HIGHEST = lax.Precision.HIGHEST
NT = (((1,), (1,)), ((), ()))
NN = (((1,), (0,)), ((), ()))


def parts_of(values):
    parts = []
    for _ in range(3):
        rounded = values.astype(jnp.bfloat16)
        parts.append(rounded)
        values = values - rounded.astype(jnp.float32)
    return parts


def store_parts(refs, at, values):
    for ref, part in zip(refs, parts_of(values)):
        ref[pl.ds(at, values.shape[0]), :] = part


def place(first, rows):
    base = first // 3
    step = lax.broadcasted_iota(jnp.int32, (rows, 1), 0) + (first - base * 3)
    third = (step * 21846) >> 16
    return step - third * 3, base + third


def hot(mask):
    return jnp.where(mask, 1.0, 0.0).astype(jnp.bfloat16)


def hot_place(first, rows):
    channel, pixel = place(first, rows)
    lane = lax.broadcasted_iota(jnp.int32, (rows, 256), 1)
    tail = lax.broadcasted_iota(jnp.int32, (rows, 128), 1)
    in_tail = (tail == (pixel >> 8)) | (tail == channel + ROWS_USED)
    return jnp.concatenate([hot(lane == (pixel & 255)), hot(in_tail)], axis=1)


def hot_token(ids):
    return hot(lax.broadcasted_iota(jnp.int32, (ids.shape[0], VOCAB), 1) == ids)


def pick(picks, parts):
    total = None
    for part in reversed(parts):
        piece = lax.dot_general(picks, part, NN, preferred_element_type=jnp.float32)
        total = piece if total is None else total + piece
    return total


def normalized(total):
    center = total - jnp.mean(total, axis=-1, keepdims=True)
    spread = jnp.mean(center * center, axis=-1, keepdims=True)
    return center * lax.rsqrt(spread + 1e-05)


def low_lanes(rows):
    return lax.broadcasted_iota(jnp.int32, (rows, 2 * HD), 1) < HD


def pair(low, first, second, head):
    if head == 0:
        return jnp.where(low, first, pltpu.roll(second, HD, 1))
    return jnp.where(low, pltpu.roll(first, HD, 1), second)


def tables_kernel(token, row, col, chan, t1, t2, t3, p1, p2, p3, where_sum):
    tokens, places = (t1, t2, t3), (p1, p2, p3)
    for at in (0, 128):
        store_parts(tokens, at, token[pl.ds(at, 128), :])
        store_parts(places, at, col[pl.ds(at, 128), :])
    rest = jnp.zeros((128 - ROWS_USED - 3, token.shape[1]), jnp.float32)
    store_parts(places, 256, jnp.concatenate([row[...], chan[...], rest], axis=0))
    where_sum[...] = pick(hot_place(POSITIONS - LAT, LAT), [p[...] for p in places])


def keys_kernel(index, ids, t1, t2, t3, p1, p2, p3, w_key, w_value, key_cat, value_cat):
    size = ids.shape[0]
    first = index[0] * POS_DEV + pl.program_id(0) * size
    total = pick(hot_place(first, size), [p1[...], p2[...], p3[...]])
    total = total + pick(hot_token(ids[...]), [t1[...], t2[...], t3[...]])
    emb = normalized(total)
    both = jnp.dot(emb, jnp.concatenate([w_key[...], w_value[...]], axis=1), precision=HIGHEST)
    keys, values = both[:, :128], both[:, 128:]
    low = low_lanes(size)
    k = [part.astype(jnp.float32) for part in parts_of(keys)]
    v = [part.astype(jnp.float32) for part in parts_of(values)]
    ones = jnp.ones_like(values)
    for head in range(2):
        both = pair(low, k[0], k[1], head)
        pieces = [both, both, pair(low, k[2], k[0], head), pair(low, k[2], k[1], head)]
        for i, piece in enumerate(pieces):
            key_cat[head, :, i * 128 : (i + 1) * 128] = piece.astype(jnp.bfloat16)
        tail = jnp.where(low, v[2], ones) if head == 0 else jnp.where(low, ones, v[2])
        value_cat[head, :, 0:128] = pair(low, v[0], v[1], head).astype(jnp.bfloat16)
        value_cat[head, :, 128:256] = tail.astype(jnp.bfloat16)


def attend_kernel(index, ids, where_sum, t1, t2, t3, w_query, key_cat, value_cat, out, attended):
    block = pl.program_id(0)
    size = ids.shape[0]
    emb = normalized(where_sum[...] + pick(hot_token(ids[...]), [t1[...], t2[...], t3[...]]))
    e = parts_of(emb)
    w = parts_of(w_query[...])
    near_w = jnp.concatenate([w[0], w[1]], axis=1)
    wide = jnp.dot(e[0], near_w, preferred_element_type=jnp.float32)
    wide = wide + jnp.dot(e[1], near_w, preferred_element_type=jnp.float32)
    wide = wide[:, :128] + wide[:, 128:]
    wide = wide + jnp.dot(
        jnp.concatenate([e[0], e[2]], axis=1),
        jnp.concatenate([w[2], w[0]], axis=0),
        preferred_element_type=jnp.float32,
    )
    queries = wide * HD ** (-0.5)
    q = [part.astype(jnp.float32) for part in parts_of(queries)]
    low = low_lanes(size)
    where = index[0] * POS_DEV + lax.broadcasted_iota(jnp.int32, (size, POS_DEV), 1)
    latent = POSITIONS - LAT + block * size + lax.broadcasted_iota(jnp.int32, (size, POS_DEV), 0)
    seen = where <= latent
    sums, weights, tops = [], [], []
    for head in range(2):
        query_cat = jnp.concatenate(
            [pair(low, q[0], q[0], head), pair(low, q[1], q[1], head)]
            + [pair(low, q[0], q[2], head), pair(low, q[1], q[2], head)],
            axis=1,
        ).astype(jnp.bfloat16)
        scores = lax.dot_general(query_cat, key_cat[head], NT, preferred_element_type=jnp.float32)
        scores = jnp.where(seen, scores, -1e30)
        top = jnp.max(scores, axis=-1, keepdims=True)
        probs = jnp.exp(scores - top)
        near = probs.astype(jnp.bfloat16)
        rest = (probs - near.astype(jnp.float32)).astype(jnp.bfloat16)
        value = value_cat[head]
        both = jnp.dot(near, value, preferred_element_type=jnp.float32)
        both = both + jnp.dot(rest, value, preferred_element_type=jnp.float32)
        lead, tail = both[:, :128], both[:, 128:]
        sums.append(lead + pltpu.roll(lead, HD, 1) + tail)
        weights.append(pltpu.roll(tail, HD, 1))
        tops.append(top)
    weight = jnp.where(low, weights[0], weights[1])
    level = jnp.where(low, tops[0], tops[1]) + jnp.log(weight)
    attended[...] = jnp.where(low, sums[0], sums[1]) / weight
    chunks = size // 8
    for r in range(8):
        out[pl.ds(r, chunks, stride=9), :] = attended[pl.ds(r, chunks, stride=8), :]
    level = level.reshape(chunks, 8, 128)
    lane = lax.broadcasted_iota(jnp.int32, level.shape, 2)
    lat = lax.broadcasted_iota(jnp.int32, level.shape, 1)
    out[pl.ds(8, chunks, stride=9), :] = jnp.sum(jnp.where((lane & 7) == lat, level, 0.0), axis=1)


def prepare_kernel(weights, out_cat, in_cat, down_cat):
    for c in range(8):
        rows = pl.ds(c * 128, 128)
        near, rest, _ = parts_of(weights[:, c * 32 : c * 32 + 16, :].reshape(128, 128))
        out_cat[rows, 0:128] = near
        out_cat[rows, 128:256] = rest
        near, rest, _ = parts_of(weights[:, c * 32 + 16 : c * 32 + 32, :].reshape(128, 128))
        near, rest = near.astype(jnp.float32), rest.astype(jnp.float32)
        low = low_lanes(128)
        in_cat[rows, :] = pair(low, near, rest, 0).astype(jnp.bfloat16)
        down = pair(low, near, rest, 1)
        down_cat[rows, 0:128] = down.astype(jnp.bfloat16)
        down_cat[rows, 128:256] = down.astype(jnp.bfloat16)


def project_kernel(states, out_cat, out):
    levels = states[pl.ds(8, 64, stride=9), :]
    low = low_lanes(64)
    rows = []
    for r in range(8):
        level = jnp.where(low, levels[:, r : r + 1], levels[:, HD + r : HD + r + 1])
        share = jnp.exp(level - jnp.max(level, axis=0, keepdims=True))
        value = jnp.sum(share * states[pl.ds(r, 64, stride=9), :], axis=0, keepdims=True)
        rows.append(value / jnp.sum(share, axis=0, keepdims=True))
    near, rest, _ = parts_of(jnp.concatenate(rows, axis=0))
    near, rest = near.astype(jnp.float32), rest.astype(jnp.float32)
    left = jnp.concatenate(
        [jnp.concatenate([near, near], axis=1), jnp.concatenate([rest, rest], axis=1)], axis=0
    ).astype(jnp.bfloat16)
    both = lax.dot_general(left, out_cat[...], NT, preferred_element_type=jnp.float32)
    partial = both[0:8] + both[8:16]
    for c in range(8):
        out[pl.ds(c, 8, stride=8), :] = partial[:, c * 128 : (c + 1) * 128]


def latent_kernel(rows, in_cat, down_cat, out):
    row = jnp.concatenate([rows[pl.ds(c, 64, stride=8), :] for c in range(8)], axis=1)
    near, rest, _ = parts_of(normalized(row))
    raw = jnp.dot(
        jnp.concatenate([near, rest], axis=0), in_cat[...], preferred_element_type=jnp.float32
    )
    raw = raw[0:64] + raw[64:128]
    hidden = jax.nn.gelu(raw + pltpu.roll(raw, HD, 1))
    near, rest, _ = parts_of(hidden)
    left = jnp.concatenate([near, rest], axis=1)
    down = lax.dot_general(left, down_cat[...], NT, preferred_element_type=jnp.float32)
    for c in range(8):
        out[pl.ds(c, 64, stride=8), :] = down[:, c * 128 : (c + 1) * 128]


VMEM = pl.BlockSpec(memory_space=pltpu.VMEM)
SMEM = pl.BlockSpec(memory_space=pltpu.SMEM)


def shape(*dims):
    return jax.ShapeDtypeStruct(dims, jnp.float32)


def params(**more):
    return pltpu.CompilerParams(vmem_limit_bytes=56 * 1024 * 1024, **more)


def exchange(value, axes):
    return lax.all_to_all(value, axes, 0, 0)


def per_device(token_ids, token_table, row_table, col_table, chan_table, w_query, w_key, w_value, w_out, w_in, w_down):
    index = lax.axis_index(POS).astype(jnp.int32).reshape(1)

    bf16 = lambda *dims: jax.ShapeDtypeStruct(dims, jnp.bfloat16)
    whole = lambda *dims: pl.BlockSpec(dims, lambda i: (0,) * len(dims))
    slab = lambda *dims: pl.BlockSpec(dims, lambda i: (i,) + (0,) * (len(dims) - 1))
    lanes = lambda *dims: pl.BlockSpec(dims, lambda i: (0, i))
    middle = lambda *dims: pl.BlockSpec(dims, lambda i: (0, i, 0))

    with jax.named_scope("weights"):
        own_ids = token_ids[POS_DEV - LAT :].astype(jnp.float32).reshape(4, 128)
        own_ids = jnp.concatenate([own_ids, jnp.zeros((4, 128), jnp.float32)], axis=0)
        own_in = w_in.reshape(16, 8, 64).transpose(1, 0, 2)
        own_down = w_down.reshape(8, 64, 16).transpose(0, 2, 1)
        packed = jnp.concatenate(
            [
                jnp.broadcast_to(w_out.T[None], (8, 16, 128)),
                jnp.concatenate([own_in, own_down], axis=2),
                jnp.broadcast_to(own_ids[None], (8, 8, 128)),
            ],
            axis=1,
        )
        packed = exchange(packed, "z")

    width = 256
    tables = pl.pallas_call(
        tables_kernel,
        grid=(D // width,),
        in_specs=[lanes(VOCAB, width), lanes(ROWS_USED, width), lanes(IMG, width), lanes(3, width)],
        out_specs=[lanes(VOCAB, width)] * 3 + [lanes(384, width)] * 3 + [lanes(LAT, width)],
        out_shape=[bf16(VOCAB, D)] * 3 + [bf16(384, D)] * 3 + [shape(LAT, D)],
        compiler_params=params(),
        cost_estimate=pl.CostEstimate(flops=2 * 10**9, transcendentals=0, bytes_accessed=8 * 10**6),
        name="tables",
    )(token_table, row_table, col_table, chan_table)
    packed, tables = lax.optimization_barrier((packed, tables))
    *splits, where_sum = tables
    tokens = splits[:3]

    with jax.named_scope("columns"):
        packed = jnp.concatenate([packed[:, :32, :].reshape(256, 128), packed[7, 32:, :]], axis=0)
        weights = exchange(jnp.broadcast_to(packed[None], (8, 264, 128)), COLUMN)
        latent_ids = weights[7, 256:260, :].astype(jnp.int32).reshape(LAT, 1)

    block = POS_DEV // KEY_STEPS
    key_cat, value_cat = pl.pallas_call(
        keys_kernel,
        grid=(KEY_STEPS,),
        in_specs=[SMEM, slab(block, 1)] + [whole(VOCAB, D)] * 3 + [whole(384, D)] * 3 + [whole(D, 128)] * 2,
        out_specs=[middle(2, block, 512), middle(2, block, 256)],
        out_shape=[bf16(2, POS_DEV, 512), bf16(2, POS_DEV, 256)],
        compiler_params=params(),
        cost_estimate=pl.CostEstimate(flops=8 * 10**9, transcendentals=0, bytes_accessed=10**7),
        name="keys",
    )(index, token_ids.reshape(POS_DEV, 1), *splits, w_key, w_value)

    size = LAT // LATENT_STEPS
    states = pl.pallas_call(
        attend_kernel,
        grid=(LATENT_STEPS,),
        in_specs=[SMEM, slab(size, 1), slab(size, D)]
        + [whole(VOCAB, D)] * 3
        + [whole(D, 128), whole(2, POS_DEV, 512), whole(2, POS_DEV, 256)],
        out_specs=slab(size // 8 * 9, 128),
        out_shape=shape(64 * 9, 128),
        scratch_shapes=[pltpu.VMEM((size, 128), jnp.float32)],
        compiler_params=params(),
        cost_estimate=pl.CostEstimate(flops=6 * 10**9, transcendentals=10**6, bytes_accessed=10**7),
        name="attend",
    )(index, latent_ids, where_sum, *tokens, w_query, key_cat, value_cat)

    with jax.named_scope("states"):
        states = exchange(states.reshape(64, 1, 1152), POS).reshape(64 * 9, 128)
    out_cat, in_cat, down_cat = pl.pallas_call(
        prepare_kernel,
        in_specs=[VMEM],
        out_specs=[VMEM] * 3,
        out_shape=[bf16(D, 256), bf16(D, 128), bf16(D, 256)],
        compiler_params=params(),
        cost_estimate=pl.CostEstimate(flops=10**9, transcendentals=0, bytes_accessed=3 * 10**6),
        name="prepare",
    )(weights)
    partial_rows = pl.pallas_call(
        project_kernel,
        in_specs=[VMEM, VMEM],
        out_specs=VMEM,
        out_shape=shape(64, 128),
        compiler_params=params(),
        name="project",
    )(states, out_cat)
    with jax.named_scope("projected"):
        projected = jnp.sum(exchange(partial_rows.reshape(8, 8, 128), HEAD), axis=0)
        rows = exchange(jnp.broadcast_to(projected[None], (64, 8, 128)), SHARERS)
    outs = pl.pallas_call(
        latent_kernel,
        in_specs=[VMEM] * 3,
        out_specs=VMEM,
        out_shape=shape(512, 128),
        compiler_params=params(),
        name="latent",
    )(rows.reshape(512, 128), in_cat, down_cat)
    with jax.named_scope("result"):
        own = projected + jnp.sum(exchange(outs.reshape(64, 8, 128), SHARERS), axis=0)
        return exchange(jnp.broadcast_to(own[None], (8, 8, 128)), HEAD).reshape(8, D)


def solution(mesh):
    fine = Mesh(mesh.devices.reshape(8, 2, 4, 4, 2), ("z", "ylo", "x", "yhi", "core"))
    placed = (
        P(POS),
        P(),
        P(),
        P(),
        P(),
        P(None, HEAD),
        P(None, HEAD),
        P(None, HEAD),
        P(HEAD, POS),
        P(POS, HEAD),
        P(HEAD, POS),
    )
    return jax.shard_map(
        per_device, mesh=fine, in_specs=placed, out_specs=P(POS, None), check_vma=False
    )
```

```python
import jax
import jax.numpy as jnp
from jax import lax
from jax.experimental import pallas as pl
from jax.experimental.pallas import tpu as pltpu
from jax.sharding import Mesh
from jax.sharding import PartitionSpec as P

D = 1024
HD = 64
IMG = 256
LAT = 512
POS_DEV = 1024
POSITIONS = 65536
VOCAB = 256
ROWS_USED = 88
KEY_STEPS = 1
LATENT_STEPS = 1
KEY_PARTS = 2
QUERY_PARTS = 4

POS = ("z", "ylo", "x")
HEAD = ("yhi", "core")
COLUMN = ("ylo", "x")
SHARERS = ("z", "yhi", "core")

HIGHEST = lax.Precision.HIGHEST
NT = (((1,), (1,)), ((), ()))
NN = (((1,), (0,)), ((), ()))


def parts_of(values):
    parts = []
    for _ in range(3):
        rounded = values.astype(jnp.bfloat16)
        parts.append(rounded)
        values = values - rounded.astype(jnp.float32)
    return parts


def store_parts(refs, at, values):
    for ref, part in zip(refs, parts_of(values)):
        ref[pl.ds(at, values.shape[0]), :] = part


def place(first, rows):
    base = first // 3
    step = lax.broadcasted_iota(jnp.int32, (rows, 1), 0) + (first - base * 3)
    third = (step * 21846) >> 16
    return step - third * 3, base + third


def hot(mask):
    return jnp.where(mask, 1.0, 0.0).astype(jnp.bfloat16)


def hot_place(first, rows):
    channel, pixel = place(first, rows)
    lane = lax.broadcasted_iota(jnp.int32, (rows, 256), 1)
    tail = lax.broadcasted_iota(jnp.int32, (rows, 128), 1)
    in_tail = (tail == (pixel >> 8)) | (tail == channel + ROWS_USED)
    return jnp.concatenate([hot(lane == (pixel & 255)), hot(in_tail)], axis=1)


def id_columns(ids, size, skip):
    turned = jnp.transpose(ids)
    column = lax.broadcasted_iota(jnp.int32, turned.shape, 1)
    start = skip + pl.program_id(0) * (size // 128)
    picked = [
        jnp.sum(jnp.where(column == start + i, turned, 0.0), axis=1, keepdims=True)
        for i in range(size // 128)
    ]
    return jnp.concatenate(picked, axis=0).astype(jnp.int32)


def hot_token(ids):
    return hot(lax.broadcasted_iota(jnp.int32, (ids.shape[0], VOCAB), 1) == ids)


def pick(picks, parts):
    total = None
    for part in reversed(parts):
        piece = lax.dot_general(picks, part, NN, preferred_element_type=jnp.float32)
        total = piece if total is None else total + piece
    return total


def normalized(total):
    center = total - jnp.mean(total, axis=-1, keepdims=True)
    spread = jnp.mean(center * center, axis=-1, keepdims=True)
    return center * lax.rsqrt(spread + 1e-05)


def low_lanes(rows):
    return lax.broadcasted_iota(jnp.int32, (rows, 2 * HD), 1) < HD


def pair(low, first, second, head):
    if head == 0:
        return jnp.where(low, first, pltpu.roll(second, HD, 1))
    return jnp.where(low, pltpu.roll(first, HD, 1), second)


def pack_kernel(ids, w_out, w_in, w_down, packed):
    low = low_lanes(16)
    own_ids = ids[...].astype(jnp.float32)
    for b in range(8):
        lanes = slice(b // 2 * 128, b // 2 * 128 + 128)
        packed[b, 0:16, :] = w_out[...]
        packed[b, 16:32, :] = pair(low, w_in[:, lanes], w_down[:, lanes], b % 2)
        packed[b, 32:40, :] = own_ids


def tables_kernel(token, row, col, chan, t1, t2, t3, p1, p2, p3, where_sum):
    tokens, places = (t1, t2, t3), (p1, p2, p3)
    for at in (0, 128):
        store_parts(tokens, at, token[pl.ds(at, 128), :])
        store_parts(places, at, col[pl.ds(at, 128), :])
    rest = jnp.zeros((128 - ROWS_USED - 3, token.shape[1]), jnp.float32)
    store_parts(places, 256, jnp.concatenate([row[...], chan[...], rest], axis=0))
    where_sum[...] = pick(hot_place(POSITIONS - LAT, LAT), [p[...] for p in places])


def keys_kernel(index, ids, t1, t2, t3, p1, p2, p3, w_key, w_value, key_cat, value_cat):
    size = POS_DEV // KEY_STEPS
    part_size = size // KEY_PARTS
    first = index[0] * POS_DEV + pl.program_id(0) * size
    columns = id_columns(ids[...].astype(jnp.float32), size, 0)
    places = [p1[...], p2[...], p3[...]]
    tokens = [t1[...], t2[...], t3[...]]
    embs = []
    for i in range(KEY_PARTS):
        total = pick(hot_place(first + i * part_size, part_size), places)
        total = total + pick(hot_token(columns[i * part_size : (i + 1) * part_size]), tokens)
        embs.append(normalized(total))
    wide = jnp.concatenate([w_key[...], w_value[...]], axis=1)
    both = jnp.concatenate([jnp.dot(emb, wide, precision=HIGHEST) for emb in embs], axis=0)
    keys, values = both[:, :128], both[:, 128:]
    low = low_lanes(size)
    k = [part.astype(jnp.float32) for part in parts_of(keys)]
    v = [part.astype(jnp.float32) for part in parts_of(values)]
    ones = jnp.ones_like(values)
    for head in range(2):
        both = pair(low, k[0], k[1], head)
        pieces = [both, both, pair(low, k[2], k[0], head), pair(low, k[2], k[1], head)]
        for i, piece in enumerate(pieces):
            key_cat[head, :, i * 128 : (i + 1) * 128] = piece.astype(jnp.bfloat16)
        tail = jnp.where(low, v[2], ones) if head == 0 else jnp.where(low, ones, v[2])
        value_cat[head, :, 0:128] = pair(low, v[0], v[1], head).astype(jnp.bfloat16)
        value_cat[head, :, 128:256] = tail.astype(jnp.bfloat16)


def attend_kernel(index, ids, where_sum, t1, t2, t3, w_query, key_cat, value_cat, out, attended):
    block = pl.program_id(0)
    size = where_sum.shape[0]
    columns = id_columns(ids[...], size, (POS_DEV - LAT) // 128)
    tokens = [t1[...], t2[...], t3[...]]
    w = parts_of(w_query[...])
    near_w = jnp.concatenate([w[0], w[1]], axis=1)
    far_w = jnp.concatenate([w[2], w[0]], axis=0)
    part_size = size // QUERY_PARTS
    queries = []
    for i in range(QUERY_PARTS):
        rows = slice(i * part_size, (i + 1) * part_size)
        e = parts_of(normalized(where_sum[rows] + pick(hot_token(columns[rows]), tokens)))
        wide = jnp.dot(e[0], near_w, preferred_element_type=jnp.float32)
        wide = wide + jnp.dot(e[1], near_w, preferred_element_type=jnp.float32)
        wide = wide[:, :128] + wide[:, 128:]
        queries.append(
            wide
            + jnp.dot(
                jnp.concatenate([e[0], e[2]], axis=1), far_w, preferred_element_type=jnp.float32
            )
        )
    queries = jnp.concatenate(queries, axis=0) * HD ** (-0.5)
    q = [part.astype(jnp.float32) for part in parts_of(queries)]
    low = low_lanes(size)
    where = index[0] * POS_DEV + lax.broadcasted_iota(jnp.int32, (size, POS_DEV), 1)
    latent = POSITIONS - LAT + block * size + lax.broadcasted_iota(jnp.int32, (size, POS_DEV), 0)
    seen = where <= latent
    sums, weights, tops = [], [], []
    for head in range(2):
        query_cat = jnp.concatenate(
            [pair(low, q[0], q[0], head), pair(low, q[1], q[1], head)]
            + [pair(low, q[0], q[2], head), pair(low, q[1], q[2], head)],
            axis=1,
        ).astype(jnp.bfloat16)
        scores = lax.dot_general(query_cat, key_cat[head], NT, preferred_element_type=jnp.float32)
        scores = jnp.where(seen, scores, -1e30)
        top = jnp.max(scores, axis=-1, keepdims=True)
        probs = jnp.exp(scores - top)
        near = probs.astype(jnp.bfloat16)
        rest = (probs - near.astype(jnp.float32)).astype(jnp.bfloat16)
        value = value_cat[head]
        both = jnp.dot(near, value, preferred_element_type=jnp.float32)
        both = both + jnp.dot(rest, value, preferred_element_type=jnp.float32)
        lead, tail = both[:, :128], both[:, 128:]
        sums.append(lead + pltpu.roll(lead, HD, 1) + tail)
        weights.append(pltpu.roll(tail, HD, 1))
        tops.append(top)
    weight = jnp.where(low, weights[0], weights[1])
    level = jnp.where(low, tops[0], tops[1]) + jnp.log(weight)
    attended[...] = jnp.where(low, sums[0], sums[1]) / weight
    chunks = size // 8
    for r in range(8):
        out[pl.ds(r, chunks, stride=9), :] = attended[pl.ds(r, chunks, stride=8), :]
    level = level.reshape(chunks, 8, 128)
    lane = lax.broadcasted_iota(jnp.int32, level.shape, 2)
    lat = lax.broadcasted_iota(jnp.int32, level.shape, 1)
    out[pl.ds(8, chunks, stride=9), :] = jnp.sum(jnp.where((lane & 7) == lat, level, 0.0), axis=1)


def prepare_kernel(weights, out_cat, in_cat, down_cat):
    for c in range(8):
        rows = pl.ds(c * 128, 128)
        near, rest, _ = parts_of(weights[:, c * 32 : c * 32 + 16, :].reshape(128, 128))
        out_cat[rows, 0:128] = near
        out_cat[rows, 128:256] = rest
        near, rest, _ = parts_of(weights[:, c * 32 + 16 : c * 32 + 32, :].reshape(128, 128))
        near, rest = near.astype(jnp.float32), rest.astype(jnp.float32)
        low = low_lanes(128)
        in_cat[rows, :] = pair(low, near, rest, 0).astype(jnp.bfloat16)
        down = pair(low, near, rest, 1)
        down_cat[rows, 0:128] = down.astype(jnp.bfloat16)
        down_cat[rows, 128:256] = down.astype(jnp.bfloat16)


def project_kernel(states, out_cat, out):
    levels = states[pl.ds(8, 64, stride=9), :]
    low = low_lanes(64)
    rows = []
    for r in range(8):
        level = jnp.where(low, levels[:, r : r + 1], levels[:, HD + r : HD + r + 1])
        share = jnp.exp(level - jnp.max(level, axis=0, keepdims=True))
        value = jnp.sum(share * states[pl.ds(r, 64, stride=9), :], axis=0, keepdims=True)
        rows.append(value / jnp.sum(share, axis=0, keepdims=True))
    near, rest, _ = parts_of(jnp.concatenate(rows, axis=0))
    near, rest = near.astype(jnp.float32), rest.astype(jnp.float32)
    left = jnp.concatenate(
        [jnp.concatenate([near, near], axis=1), jnp.concatenate([rest, rest], axis=1)], axis=0
    ).astype(jnp.bfloat16)
    both = lax.dot_general(left, out_cat[...], NT, preferred_element_type=jnp.float32)
    partial = both[0:8] + both[8:16]
    for c in range(8):
        out[pl.ds(c, 8, stride=8), :] = partial[:, c * 128 : (c + 1) * 128]


def latent_kernel(rows, in_cat, down_cat, out):
    row = jnp.concatenate([rows[pl.ds(c, 64, stride=8), :] for c in range(8)], axis=1)
    near, rest, _ = parts_of(normalized(row))
    raw = jnp.dot(
        jnp.concatenate([near, rest], axis=0), in_cat[...], preferred_element_type=jnp.float32
    )
    raw = raw[0:64] + raw[64:128]
    hidden = jax.nn.gelu(raw + pltpu.roll(raw, HD, 1))
    near, rest, _ = parts_of(hidden)
    left = jnp.concatenate([near, rest], axis=1)
    down = lax.dot_general(left, down_cat[...], NT, preferred_element_type=jnp.float32)
    for c in range(8):
        out[pl.ds(c, 64, stride=8), :] = down[:, c * 128 : (c + 1) * 128]


VMEM = pl.BlockSpec(memory_space=pltpu.VMEM)
SMEM = pl.BlockSpec(memory_space=pltpu.SMEM)


def shape(*dims):
    return jax.ShapeDtypeStruct(dims, jnp.float32)


def params(**more):
    return pltpu.CompilerParams(vmem_limit_bytes=56 * 1024 * 1024, **more)


def exchange(value, axes):
    return lax.all_to_all(value, axes, 0, 0)


def per_device(token_ids, token_table, row_table, col_table, chan_table, w_query, w_key, w_value, w_out, w_in, w_down):
    index = lax.axis_index(POS).astype(jnp.int32).reshape(1)

    bf16 = lambda *dims: jax.ShapeDtypeStruct(dims, jnp.bfloat16)
    whole = lambda *dims: pl.BlockSpec(dims, lambda i: (0,) * len(dims))
    slab = lambda *dims: pl.BlockSpec(dims, lambda i: (i,) + (0,) * (len(dims) - 1))
    lanes = lambda *dims: pl.BlockSpec(dims, lambda i: (0, i))
    middle = lambda *dims: pl.BlockSpec(dims, lambda i: (0, i, 0))

    with jax.named_scope("weights"):
        packed = pl.pallas_call(
            pack_kernel,
            in_specs=[VMEM] * 4,
            out_specs=VMEM,
            out_shape=shape(8, 40, 128),
            compiler_params=params(),
            name="pack",
        )(token_ids.reshape(8, 128), w_out.T, w_in, w_down.T)
        packed = exchange(packed, "z")

    width = 256
    tables = pl.pallas_call(
        tables_kernel,
        grid=(D // width,),
        in_specs=[lanes(VOCAB, width), lanes(ROWS_USED, width), lanes(IMG, width), lanes(3, width)],
        out_specs=[lanes(VOCAB, width)] * 3 + [lanes(384, width)] * 3 + [lanes(LAT, width)],
        out_shape=[bf16(VOCAB, D)] * 3 + [bf16(384, D)] * 3 + [shape(LAT, D)],
        compiler_params=params(),
        cost_estimate=pl.CostEstimate(flops=2 * 10**9, transcendentals=0, bytes_accessed=8 * 10**6),
        name="tables",
    )(token_table, row_table, col_table, chan_table)
    packed, tables = lax.optimization_barrier((packed, tables))
    *splits, where_sum = tables
    tokens = splits[:3]

    with jax.named_scope("columns"):
        packed = jnp.concatenate([packed[:, :32, :].reshape(256, 128), packed[7, 32:, :]], axis=0)
        weights = exchange(jnp.broadcast_to(packed[None], (8, 264, 128)), COLUMN)

    block = POS_DEV // KEY_STEPS
    key_cat, value_cat = pl.pallas_call(
        keys_kernel,
        grid=(KEY_STEPS,),
        in_specs=[SMEM, whole(8, 128)] + [whole(VOCAB, D)] * 3 + [whole(384, D)] * 3 + [whole(D, 128)] * 2,
        out_specs=[middle(2, block, 512), middle(2, block, 256)],
        out_shape=[bf16(2, POS_DEV, 512), bf16(2, POS_DEV, 256)],
        compiler_params=params(),
        cost_estimate=pl.CostEstimate(flops=8 * 10**9, transcendentals=0, bytes_accessed=10**7),
        name="keys",
    )(index, token_ids.reshape(8, 128), *splits, w_key, w_value)

    size = LAT // LATENT_STEPS
    states = pl.pallas_call(
        attend_kernel,
        grid=(LATENT_STEPS,),
        in_specs=[SMEM, whole(8, 128), slab(size, D)]
        + [whole(VOCAB, D)] * 3
        + [whole(D, 128), whole(2, POS_DEV, 512), whole(2, POS_DEV, 256)],
        out_specs=slab(size // 8 * 9, 128),
        out_shape=shape(64 * 9, 128),
        scratch_shapes=[pltpu.VMEM((size, 128), jnp.float32)],
        compiler_params=params(),
        cost_estimate=pl.CostEstimate(flops=6 * 10**9, transcendentals=10**6, bytes_accessed=10**7),
        name="attend",
    )(index, weights[7, 256:264, :], where_sum, *tokens, w_query, key_cat, value_cat)

    with jax.named_scope("states"):
        states = exchange(states.reshape(64, 1, 1152), POS).reshape(64 * 9, 128)
    out_cat, in_cat, down_cat = pl.pallas_call(
        prepare_kernel,
        in_specs=[VMEM],
        out_specs=[VMEM] * 3,
        out_shape=[bf16(D, 256), bf16(D, 128), bf16(D, 256)],
        compiler_params=params(),
        cost_estimate=pl.CostEstimate(flops=10**9, transcendentals=0, bytes_accessed=3 * 10**6),
        name="prepare",
    )(weights)
    partial_rows = pl.pallas_call(
        project_kernel,
        in_specs=[VMEM, VMEM],
        out_specs=VMEM,
        out_shape=shape(64, 128),
        compiler_params=params(),
        name="project",
    )(states, out_cat)
    with jax.named_scope("projected"):
        projected = jnp.sum(exchange(partial_rows.reshape(8, 8, 128), HEAD), axis=0)
        rows = exchange(jnp.broadcast_to(projected[None], (64, 8, 128)), SHARERS)
    outs = pl.pallas_call(
        latent_kernel,
        in_specs=[VMEM] * 3,
        out_specs=VMEM,
        out_shape=shape(512, 128),
        compiler_params=params(),
        name="latent",
    )(rows.reshape(512, 128), in_cat, down_cat)
    with jax.named_scope("result"):
        own = projected + jnp.sum(exchange(outs.reshape(64, 8, 128), SHARERS), axis=0)
        return exchange(jnp.broadcast_to(own[None], (8, 8, 128)), HEAD).reshape(8, D)


def solution(mesh):
    fine = Mesh(mesh.devices.reshape(8, 2, 4, 4, 2), ("z", "ylo", "x", "yhi", "core"))
    placed = (
        P(POS),
        P(),
        P(),
        P(),
        P(),
        P(None, HEAD),
        P(None, HEAD),
        P(None, HEAD),
        P(HEAD, POS),
        P(POS, HEAD),
        P(HEAD, POS),
    )
    return jax.shard_map(
        per_device, mesh=fine, in_specs=placed, out_specs=P(POS, None), check_vma=False
    )
```

```python
import jax
import jax.numpy as jnp
from jax import lax
from jax.experimental import pallas as pl
from jax.experimental.pallas import tpu as pltpu
from jax.sharding import Mesh
from jax.sharding import PartitionSpec as P

D = 1024
HD = 64
IMG = 256
LAT = 512
POS_DEV = 1024
POSITIONS = 65536
VOCAB = 256
ROWS_USED = 88
KEY_STEPS = 1
LATENT_STEPS = 2
KEY_PARTS = 2
QUERY_PARTS = 1

POS = ("z", "ylo", "x")
HEAD = ("yhi", "core")
COLUMN = ("ylo", "x")

HIGHEST = lax.Precision.HIGHEST
NT = (((1,), (1,)), ((), ()))
NN = (((1,), (0,)), ((), ()))


def parts_of(values):
    parts = []
    for _ in range(3):
        rounded = values.astype(jnp.bfloat16)
        parts.append(rounded)
        values = values - rounded.astype(jnp.float32)
    return parts


def store_parts(refs, at, values):
    for ref, part in zip(refs, parts_of(values)):
        ref[pl.ds(at, values.shape[0]), :] = part


def place(first, rows):
    base = first // 3
    step = lax.broadcasted_iota(jnp.int32, (rows, 1), 0) + (first - base * 3)
    third = (step * 21846) >> 16
    return step - third * 3, base + third


def hot(mask):
    return jnp.where(mask, 1.0, 0.0).astype(jnp.bfloat16)


def hot_place(first, rows):
    channel, pixel = place(first, rows)
    lane = lax.broadcasted_iota(jnp.int32, (rows, 256), 1)
    tail = lax.broadcasted_iota(jnp.int32, (rows, 128), 1)
    in_tail = (tail == (pixel >> 8)) | (tail == channel + ROWS_USED)
    return jnp.concatenate([hot(lane == (pixel & 255)), hot(in_tail)], axis=1)


def id_columns(ids, size, skip):
    turned = jnp.transpose(ids)
    column = lax.broadcasted_iota(jnp.int32, turned.shape, 1)
    start = skip + pl.program_id(0) * (size // 128)
    picked = [
        jnp.sum(jnp.where(column == start + i, turned, 0.0), axis=1, keepdims=True)
        for i in range(size // 128)
    ]
    return jnp.concatenate(picked, axis=0).astype(jnp.int32)


def hot_token(ids):
    return hot(lax.broadcasted_iota(jnp.int32, (ids.shape[0], VOCAB), 1) == ids)


def pick(picks, parts):
    total = None
    for part in reversed(parts):
        piece = lax.dot_general(picks, part, NN, preferred_element_type=jnp.float32)
        total = piece if total is None else total + piece
    return total


def normalized(total):
    center = total - jnp.mean(total, axis=-1, keepdims=True)
    spread = jnp.mean(center * center, axis=-1, keepdims=True)
    return center * lax.rsqrt(spread + 1e-05)


def low_lanes(rows):
    return lax.broadcasted_iota(jnp.int32, (rows, 2 * HD), 1) < HD


def pair(low, first, second, head):
    if head == 0:
        return jnp.where(low, first, pltpu.roll(second, HD, 1))
    return jnp.where(low, pltpu.roll(first, HD, 1), second)


def pack_kernel(ids, w_out, w_in, w_down, packed):
    low = low_lanes(16)
    own_ids = ids[...].astype(jnp.float32)
    for b in range(8):
        lanes = slice(b // 2 * 128, b // 2 * 128 + 128)
        packed[b, 0:16, :] = w_out[...]
        packed[b, 16:32, :] = pair(low, w_in[:, lanes], w_down[:, lanes], b % 2)
        packed[b, 32:40, :] = own_ids


def tables_kernel(token, row, col, chan, t1, t2, t3, p1, p2, p3, where_sum):
    tokens, places = (t1, t2, t3), (p1, p2, p3)
    for at in (0, 128):
        store_parts(tokens, at, token[pl.ds(at, 128), :])
        store_parts(places, at, col[pl.ds(at, 128), :])
    rest = jnp.zeros((128 - ROWS_USED - 3, token.shape[1]), jnp.float32)
    store_parts(places, 256, jnp.concatenate([row[...], chan[...], rest], axis=0))
    where_sum[...] = pick(hot_place(POSITIONS - LAT, LAT), [p[...] for p in places])


def keys_kernel(index, ids, t1, t2, t3, p1, p2, p3, w_key, w_value, key_cat, value_cat):
    size = POS_DEV // KEY_STEPS
    part_size = size // KEY_PARTS
    first = index[0] * POS_DEV + pl.program_id(0) * size
    columns = id_columns(ids[...].astype(jnp.float32), size, 0)
    places = [p1[...], p2[...], p3[...]]
    tokens = [t1[...], t2[...], t3[...]]
    embs = []
    for i in range(KEY_PARTS):
        total = pick(hot_place(first + i * part_size, part_size), places)
        total = total + pick(hot_token(columns[i * part_size : (i + 1) * part_size]), tokens)
        embs.append(normalized(total))
    wide = jnp.concatenate([w_key[...], w_value[...]], axis=1)
    both = jnp.concatenate([jnp.dot(emb, wide, precision=HIGHEST) for emb in embs], axis=0)
    keys, values = both[:, :128], both[:, 128:]
    low = low_lanes(size)
    k = [part.astype(jnp.float32) for part in parts_of(keys)]
    v = [part.astype(jnp.float32) for part in parts_of(values)]
    ones = jnp.ones_like(values)
    for head in range(2):
        both = pair(low, k[0], k[1], head)
        pieces = [both, both, pair(low, k[2], k[0], head), pair(low, k[2], k[1], head)]
        for i, piece in enumerate(pieces):
            key_cat[head, :, i * 128 : (i + 1) * 128] = piece.astype(jnp.bfloat16)
        tail = jnp.where(low, v[2], ones) if head == 0 else jnp.where(low, ones, v[2])
        value_cat[head, :, 0:128] = pair(low, v[0], v[1], head).astype(jnp.bfloat16)
        value_cat[head, :, 128:256] = tail.astype(jnp.bfloat16)


def attend_kernel(index, ids, where_sum, t1, t2, t3, w_query, key_cat, value_cat, out, attended):
    block = pl.program_id(0)
    size = where_sum.shape[0]
    columns = id_columns(ids[...], size, (POS_DEV - LAT) // 128)
    tokens = [t1[...], t2[...], t3[...]]
    w = parts_of(w_query[...])
    near_w = jnp.concatenate([w[0], w[1]], axis=1)
    far_w = jnp.concatenate([w[2], w[0]], axis=0)
    part_size = size // QUERY_PARTS
    queries = []
    for i in range(QUERY_PARTS):
        rows = slice(i * part_size, (i + 1) * part_size)
        e = parts_of(normalized(where_sum[rows] + pick(hot_token(columns[rows]), tokens)))
        wide = jnp.dot(e[0], near_w, preferred_element_type=jnp.float32)
        wide = wide + jnp.dot(e[1], near_w, preferred_element_type=jnp.float32)
        wide = wide[:, :128] + wide[:, 128:]
        queries.append(
            wide
            + jnp.dot(
                jnp.concatenate([e[0], e[2]], axis=1), far_w, preferred_element_type=jnp.float32
            )
        )
    queries = jnp.concatenate(queries, axis=0) * HD ** (-0.5)
    q = [part.astype(jnp.float32) for part in parts_of(queries)]
    low = low_lanes(size)
    where = index[0] * POS_DEV + lax.broadcasted_iota(jnp.int32, (size, POS_DEV), 1)
    latent = POSITIONS - LAT + block * size + lax.broadcasted_iota(jnp.int32, (size, POS_DEV), 0)
    seen = where <= latent
    sums, weights, tops = [], [], []
    for head in range(2):
        query_cat = jnp.concatenate(
            [pair(low, q[0], q[0], head), pair(low, q[1], q[1], head)]
            + [pair(low, q[0], q[2], head), pair(low, q[1], q[2], head)],
            axis=1,
        ).astype(jnp.bfloat16)
        scores = lax.dot_general(query_cat, key_cat[head], NT, preferred_element_type=jnp.float32)
        scores = jnp.where(seen, scores, -1e30)
        top = jnp.max(scores, axis=-1, keepdims=True)
        probs = jnp.exp(scores - top)
        near = probs.astype(jnp.bfloat16)
        rest = (probs - near.astype(jnp.float32)).astype(jnp.bfloat16)
        value = value_cat[head]
        both = jnp.dot(near, value, preferred_element_type=jnp.float32)
        both = both + jnp.dot(rest, value, preferred_element_type=jnp.float32)
        lead, tail = both[:, :128], both[:, 128:]
        sums.append(lead + pltpu.roll(lead, HD, 1) + tail)
        weights.append(pltpu.roll(tail, HD, 1))
        tops.append(top)
    weight = jnp.where(low, weights[0], weights[1])
    level = jnp.where(low, tops[0], tops[1]) + jnp.log(weight)
    attended[...] = jnp.where(low, sums[0], sums[1]) / weight
    chunks = size // 8
    for r in range(8):
        out[pl.ds(r, chunks, stride=9), :] = attended[pl.ds(r, chunks, stride=8), :]
    level = level.reshape(chunks, 8, 128)
    lane = lax.broadcasted_iota(jnp.int32, level.shape, 2)
    lat = lax.broadcasted_iota(jnp.int32, level.shape, 1)
    out[pl.ds(8, chunks, stride=9), :] = jnp.sum(jnp.where((lane & 7) == lat, level, 0.0), axis=1)


def prepare_kernel(weights, out_cat, in_cat, down_cat):
    for c in range(8):
        rows = pl.ds(c * 128, 128)
        near, rest, _ = parts_of(weights[:, c * 32 : c * 32 + 16, :].reshape(128, 128))
        out_cat[rows, 0:128] = near
        out_cat[rows, 128:256] = rest
        near, rest, _ = parts_of(weights[:, c * 32 + 16 : c * 32 + 32, :].reshape(128, 128))
        near, rest = near.astype(jnp.float32), rest.astype(jnp.float32)
        low = low_lanes(128)
        in_cat[rows, :] = pair(low, near, rest, 0).astype(jnp.bfloat16)
        down = pair(low, near, rest, 1)
        down_cat[rows, 0:128] = down.astype(jnp.bfloat16)
        down_cat[rows, 128:256] = down.astype(jnp.bfloat16)


def project_kernel(states, out_cat, out):
    levels = states[pl.ds(8, 64, stride=9), :]
    low = low_lanes(64)
    rows = []
    for r in range(8):
        level = jnp.where(low, levels[:, r : r + 1], levels[:, HD + r : HD + r + 1])
        share = jnp.exp(level - jnp.max(level, axis=0, keepdims=True))
        value = jnp.sum(share * states[pl.ds(r, 64, stride=9), :], axis=0, keepdims=True)
        rows.append(value / jnp.sum(share, axis=0, keepdims=True))
    near, rest, _ = parts_of(jnp.concatenate(rows, axis=0))
    near, rest = near.astype(jnp.float32), rest.astype(jnp.float32)
    left = jnp.concatenate(
        [jnp.concatenate([near, near], axis=1), jnp.concatenate([rest, rest], axis=1)], axis=0
    ).astype(jnp.bfloat16)
    both = lax.dot_general(left, out_cat[...], NT, preferred_element_type=jnp.float32)
    partial = both[0:8] + both[8:16]
    for copy in range(8):
        for c in range(8):
            out[copy, pl.ds(c, 8, stride=8), :] = partial[:, c * 128 : (c + 1) * 128]


def latent_kernel(rows, in_cat, down_cat, out):
    row = jnp.concatenate([rows[pl.ds(c, 64, stride=8), :] for c in range(8)], axis=1)
    near, rest, _ = parts_of(normalized(row))
    raw = jnp.dot(
        jnp.concatenate([near, rest], axis=0), in_cat[...], preferred_element_type=jnp.float32
    )
    raw = raw[0:64] + raw[64:128]
    hidden = jax.nn.gelu(raw + pltpu.roll(raw, HD, 1))
    near, rest, _ = parts_of(hidden)
    left = jnp.concatenate([near, rest], axis=1)
    down = lax.dot_general(left, down_cat[...], NT, preferred_element_type=jnp.float32)
    for c in range(8):
        out[pl.ds(c, 64, stride=8), :] = down[:, c * 128 : (c + 1) * 128]


VMEM = pl.BlockSpec(memory_space=pltpu.VMEM)
SMEM = pl.BlockSpec(memory_space=pltpu.SMEM)


def shape(*dims):
    return jax.ShapeDtypeStruct(dims, jnp.float32)


def params(**more):
    return pltpu.CompilerParams(vmem_limit_bytes=56 * 1024 * 1024, **more)


def exchange(value, axes):
    return lax.all_to_all(value, axes, 0, 0)


def per_device(token_ids, token_table, row_table, col_table, chan_table, w_query, w_key, w_value, w_out, w_in, w_down):
    index = lax.axis_index(POS).astype(jnp.int32).reshape(1)

    bf16 = lambda *dims: jax.ShapeDtypeStruct(dims, jnp.bfloat16)
    whole = lambda *dims: pl.BlockSpec(dims, lambda i: (0,) * len(dims))
    slab = lambda *dims: pl.BlockSpec(dims, lambda i: (i,) + (0,) * (len(dims) - 1))
    lanes = lambda *dims: pl.BlockSpec(dims, lambda i: (0, i))
    middle = lambda *dims: pl.BlockSpec(dims, lambda i: (0, i, 0))

    with jax.named_scope("weights"):
        packed = pl.pallas_call(
            pack_kernel,
            in_specs=[VMEM] * 4,
            out_specs=VMEM,
            out_shape=shape(8, 40, 128),
            compiler_params=params(),
            name="pack",
        )(token_ids.reshape(8, 128), w_out.T, w_in, w_down.T)
        packed = exchange(packed, "z")

    width = 256
    tables = pl.pallas_call(
        tables_kernel,
        grid=(D // width,),
        in_specs=[lanes(VOCAB, width), lanes(ROWS_USED, width), lanes(IMG, width), lanes(3, width)],
        out_specs=[lanes(VOCAB, width)] * 3 + [lanes(384, width)] * 3 + [lanes(LAT, width)],
        out_shape=[bf16(VOCAB, D)] * 3 + [bf16(384, D)] * 3 + [shape(LAT, D)],
        compiler_params=params(),
        cost_estimate=pl.CostEstimate(flops=2 * 10**9, transcendentals=0, bytes_accessed=8 * 10**6),
        name="tables",
    )(token_table, row_table, col_table, chan_table)
    packed, tables = lax.optimization_barrier((packed, tables))
    *splits, where_sum = tables
    tokens = splits[:3]

    with jax.named_scope("columns"):
        packed = jnp.concatenate([packed[:, :32, :].reshape(256, 128), packed[7, 32:, :]], axis=0)
        weights = exchange(jnp.broadcast_to(packed[None], (8, 264, 128)), COLUMN)

    block = POS_DEV // KEY_STEPS
    key_cat, value_cat = pl.pallas_call(
        keys_kernel,
        grid=(KEY_STEPS,),
        in_specs=[SMEM, whole(8, 128)] + [whole(VOCAB, D)] * 3 + [whole(384, D)] * 3 + [whole(D, 128)] * 2,
        out_specs=[middle(2, block, 512), middle(2, block, 256)],
        out_shape=[bf16(2, POS_DEV, 512), bf16(2, POS_DEV, 256)],
        compiler_params=params(),
        cost_estimate=pl.CostEstimate(flops=8 * 10**9, transcendentals=0, bytes_accessed=10**7),
        name="keys",
    )(index, token_ids.reshape(8, 128), *splits, w_key, w_value)

    size = LAT // LATENT_STEPS
    states = pl.pallas_call(
        attend_kernel,
        grid=(LATENT_STEPS,),
        in_specs=[SMEM, whole(8, 128), slab(size, D)]
        + [whole(VOCAB, D)] * 3
        + [whole(D, 128), whole(2, POS_DEV, 512), whole(2, POS_DEV, 256)],
        out_specs=slab(size // 8 * 9, 128),
        out_shape=shape(64 * 9, 128),
        scratch_shapes=[pltpu.VMEM((size, 128), jnp.float32)],
        compiler_params=params(),
        cost_estimate=pl.CostEstimate(flops=6 * 10**9, transcendentals=10**6, bytes_accessed=10**7),
        name="attend",
    )(index, weights[7, 256:264, :], where_sum, *tokens, w_query, key_cat, value_cat)

    with jax.named_scope("states"):
        states = exchange(states.reshape(64, 1, 1152), POS).reshape(64 * 9, 128)
    out_cat, in_cat, down_cat = pl.pallas_call(
        prepare_kernel,
        in_specs=[VMEM],
        out_specs=[VMEM] * 3,
        out_shape=[bf16(D, 256), bf16(D, 128), bf16(D, 256)],
        compiler_params=params(),
        cost_estimate=pl.CostEstimate(flops=10**9, transcendentals=0, bytes_accessed=3 * 10**6),
        name="prepare",
    )(weights)
    partial_rows = pl.pallas_call(
        project_kernel,
        in_specs=[VMEM, VMEM],
        out_specs=VMEM,
        out_shape=shape(8, 64, 128),
        compiler_params=params(),
        name="project",
    )(states, out_cat)
    with jax.named_scope("projected"):
        projected = jnp.sum(exchange(partial_rows, HEAD), axis=0)
        rows = exchange(jnp.broadcast_to(projected[None], (8, 64, 128)), "z")
    outs = pl.pallas_call(
        latent_kernel,
        in_specs=[VMEM] * 3,
        out_specs=VMEM,
        out_shape=shape(512, 128),
        compiler_params=params(),
        name="latent",
    )(rows.reshape(512, 128), in_cat, down_cat)
    with jax.named_scope("result"):
        own = jnp.sum(exchange(outs.reshape(8, 64, 128), "z"), axis=0)
        total = jnp.sum(exchange(jnp.broadcast_to(own[None], (8, 64, 128)), HEAD), axis=0)
        return (projected + total).reshape(8, D)


def solution(mesh):
    fine = Mesh(mesh.devices.reshape(8, 2, 4, 4, 2), ("z", "ylo", "x", "yhi", "core"))
    placed = (
        P(POS),
        P(),
        P(),
        P(),
        P(),
        P(None, HEAD),
        P(None, HEAD),
        P(None, HEAD),
        P(HEAD, POS),
        P(POS, HEAD),
        P(HEAD, POS),
    )
    return jax.shard_map(
        per_device, mesh=fine, in_specs=placed, out_specs=P(POS, None), check_vma=False
    )
```

```python
import jax
import jax.numpy as jnp
from jax import lax
from jax.experimental import pallas as pl
from jax.experimental.pallas import tpu as pltpu
from jax.sharding import Mesh
from jax.sharding import PartitionSpec as P

D = 1024
HD = 64
IMG = 256
LAT = 512
POS_DEV = 1024
POSITIONS = 65536
VOCAB = 256
ROWS_USED = 88
KEY_STEPS = 1
LATENT_STEPS = 1
KEY_PARTS = 2
QUERY_PARTS = 2

POS = ("z", "ylo", "x")
HEAD = ("yhi", "core")
COLUMN = ("ylo", "x")

HIGHEST = lax.Precision.HIGHEST
NT = (((1,), (1,)), ((), ()))
NN = (((1,), (0,)), ((), ()))


def parts_of(values):
    parts = []
    for _ in range(3):
        rounded = values.astype(jnp.bfloat16)
        parts.append(rounded)
        values = values - rounded.astype(jnp.float32)
    return parts


def store_parts(refs, at, values):
    for ref, part in zip(refs, parts_of(values)):
        ref[pl.ds(at, values.shape[0]), :] = part


def place(first, rows):
    base = first // 3
    step = lax.broadcasted_iota(jnp.int32, (rows, 1), 0) + (first - base * 3)
    third = (step * 21846) >> 16
    return step - third * 3, base + third


def hot(mask):
    return jnp.where(mask, 1.0, 0.0).astype(jnp.bfloat16)


def hot_place(first, rows):
    channel, pixel = place(first, rows)
    lane = lax.broadcasted_iota(jnp.int32, (rows, 256), 1)
    tail = lax.broadcasted_iota(jnp.int32, (rows, 128), 1)
    in_tail = (tail == (pixel >> 8)) | (tail == channel + ROWS_USED)
    return jnp.concatenate([hot(lane == (pixel & 255)), hot(in_tail)], axis=1)


def id_columns(ids, size, skip):
    turned = jnp.transpose(ids)
    column = lax.broadcasted_iota(jnp.int32, turned.shape, 1)
    start = skip + pl.program_id(0) * (size // 128)
    picked = [
        jnp.sum(jnp.where(column == start + i, turned, 0.0), axis=1, keepdims=True)
        for i in range(size // 128)
    ]
    return jnp.concatenate(picked, axis=0).astype(jnp.int32)


def hot_token(ids):
    return hot(lax.broadcasted_iota(jnp.int32, (ids.shape[0], VOCAB), 1) == ids)


def pick(picks, parts):
    total = None
    for part in reversed(parts):
        piece = lax.dot_general(picks, part, NN, preferred_element_type=jnp.float32)
        total = piece if total is None else total + piece
    return total


def normalized(total):
    center = total - jnp.mean(total, axis=-1, keepdims=True)
    spread = jnp.mean(center * center, axis=-1, keepdims=True)
    return center * lax.rsqrt(spread + 1e-05)


def low_lanes(rows):
    return lax.broadcasted_iota(jnp.int32, (rows, 2 * HD), 1) < HD


def pair(low, first, second, head):
    if head == 0:
        return jnp.where(low, first, pltpu.roll(second, HD, 1))
    return jnp.where(low, pltpu.roll(first, HD, 1), second)


def pack_kernel(ids, w_out, w_in, w_down, packed):
    low = low_lanes(16)
    own_ids = ids[...].astype(jnp.float32)
    for b in range(8):
        lanes = slice(b // 2 * 128, b // 2 * 128 + 128)
        packed[b, 0:16, :] = w_out[...]
        packed[b, 16:32, :] = pair(low, w_in[:, lanes], w_down[:, lanes], b % 2)
        packed[b, 32:40, :] = own_ids


def tables_kernel(token, row, col, chan, t1, t2, t3, p1, p2, p3, where_sum):
    tokens, places = (t1, t2, t3), (p1, p2, p3)
    for at in (0, 128):
        store_parts(tokens, at, token[pl.ds(at, 128), :])
        store_parts(places, at, col[pl.ds(at, 128), :])
    rest = jnp.zeros((128 - ROWS_USED - 3, token.shape[1]), jnp.float32)
    store_parts(places, 256, jnp.concatenate([row[...], chan[...], rest], axis=0))
    where_sum[...] = pick(hot_place(POSITIONS - LAT, LAT), [p[...] for p in places])


def keys_kernel(index, ids, t1, t2, t3, p1, p2, p3, w_key, w_value, key_cat, value_cat):
    size = POS_DEV // KEY_STEPS
    part_size = size // KEY_PARTS
    first = index[0] * POS_DEV + pl.program_id(0) * size
    columns = id_columns(ids[...].astype(jnp.float32), size, 0)
    places = [p1[...], p2[...], p3[...]]
    tokens = [t1[...], t2[...], t3[...]]
    embs = []
    for i in range(KEY_PARTS):
        total = pick(hot_place(first + i * part_size, part_size), places)
        total = total + pick(hot_token(columns[i * part_size : (i + 1) * part_size]), tokens)
        embs.append(normalized(total))
    wide = jnp.concatenate([w_key[...], w_value[...]], axis=1)
    both = jnp.concatenate([jnp.dot(emb, wide, precision=HIGHEST) for emb in embs], axis=0)
    keys, values = both[:, :128], both[:, 128:]
    low = low_lanes(size)
    k = [part.astype(jnp.float32) for part in parts_of(keys)]
    v = [part.astype(jnp.float32) for part in parts_of(values)]
    ones = jnp.ones_like(values)
    for head in range(2):
        both = pair(low, k[0], k[1], head)
        pieces = [pair(low, k[2], k[0], head), both, pair(low, k[2], k[1], head)]
        for i, piece in enumerate(pieces):
            key_cat[head, :, i * 128 : (i + 1) * 128] = piece.astype(jnp.bfloat16)
        tail = jnp.where(low, v[2], ones) if head == 0 else jnp.where(low, ones, v[2])
        value_cat[head, :, 0:128] = pair(low, v[0], v[1], head).astype(jnp.bfloat16)
        value_cat[head, :, 128:256] = tail.astype(jnp.bfloat16)


def attend_kernel(index, ids, where_sum, t1, t2, t3, w_query, key_cat, value_cat, out, attended):
    block = pl.program_id(0)
    size = where_sum.shape[0]
    columns = id_columns(ids[...], size, (POS_DEV - LAT) // 128)
    tokens = [t1[...], t2[...], t3[...]]
    w = parts_of(w_query[...])
    near_w = jnp.concatenate([w[0], w[1]], axis=1)
    far_w = jnp.concatenate([w[2], w[0]], axis=0)
    part_size = size // QUERY_PARTS
    low = low_lanes(part_size)
    parts = [slice(i * part_size, (i + 1) * part_size) for i in range(QUERY_PARTS)]
    all_q = []
    for rows in parts:
        e = parts_of(normalized(where_sum[rows] + pick(hot_token(columns[rows]), tokens)))
        wide = jnp.dot(e[0], near_w, preferred_element_type=jnp.float32)
        wide = wide + jnp.dot(e[1], near_w, preferred_element_type=jnp.float32)
        wide = wide[:, :128] + wide[:, 128:]
        wide = wide + jnp.dot(
            jnp.concatenate([e[0], e[2]], axis=1), far_w, preferred_element_type=jnp.float32
        )
        all_q.append([part.astype(jnp.float32) for part in parts_of(wide * HD ** (-0.5))])
    levels = []
    for rows, q in zip(parts, all_q):
        where = index[0] * POS_DEV + lax.broadcasted_iota(jnp.int32, (part_size, POS_DEV), 1)
        latent = lax.broadcasted_iota(jnp.int32, (part_size, POS_DEV), 0)
        seen = where <= latent + (POSITIONS - LAT + block * size + rows.start)
        sums, weights, tops = [], [], []
        for head in range(2):
            key = key_cat[head]
            lead = jnp.concatenate([pair(low, q[0], q[2], head), pair(low, q[0], q[0], head)], axis=1)
            rest = jnp.concatenate([pair(low, q[1], q[1], head), pair(low, q[1], q[2], head)], axis=1)
            scores = lax.dot_general(
                lead.astype(jnp.bfloat16), key[:, 0:256], NT, preferred_element_type=jnp.float32
            ) + lax.dot_general(
                rest.astype(jnp.bfloat16), key[:, 128:384], NT, preferred_element_type=jnp.float32
            )
            scores = jnp.where(seen, scores, -1e30)
            top = jnp.max(scores, axis=-1, keepdims=True)
            probs = jnp.exp(scores - top)
            near = probs.astype(jnp.bfloat16)
            rest = (probs - near.astype(jnp.float32)).astype(jnp.bfloat16)
            value = value_cat[head]
            both = jnp.dot(near, value, preferred_element_type=jnp.float32)
            both = both + jnp.dot(rest, value, preferred_element_type=jnp.float32)
            lead, tail = both[:, :128], both[:, 128:]
            sums.append(lead + pltpu.roll(lead, HD, 1) + tail)
            weights.append(pltpu.roll(tail, HD, 1))
            tops.append(top)
        weight = jnp.where(low, weights[0], weights[1])
        levels.append(jnp.where(low, tops[0], tops[1]) + jnp.log(weight))
        attended[rows] = jnp.where(low, sums[0], sums[1]) / weight
    level = jnp.concatenate(levels, axis=0)
    chunks = size // 8
    for r in range(8):
        out[pl.ds(r, chunks, stride=9), :] = attended[pl.ds(r, chunks, stride=8), :]
    level = level.reshape(chunks, 8, 128)
    lane = lax.broadcasted_iota(jnp.int32, level.shape, 2)
    lat = lax.broadcasted_iota(jnp.int32, level.shape, 1)
    out[pl.ds(8, chunks, stride=9), :] = jnp.sum(jnp.where((lane & 7) == lat, level, 0.0), axis=1)


def prepare_kernel(weights, out_cat, in_cat, down_cat):
    for c in range(8):
        rows = pl.ds(c * 128, 128)
        near, rest, _ = parts_of(weights[:, c * 32 : c * 32 + 16, :].reshape(128, 128))
        out_cat[rows, 0:128] = near
        out_cat[rows, 128:256] = rest
        near, rest, _ = parts_of(weights[:, c * 32 + 16 : c * 32 + 32, :].reshape(128, 128))
        near, rest = near.astype(jnp.float32), rest.astype(jnp.float32)
        low = low_lanes(128)
        in_cat[rows, :] = pair(low, near, rest, 0).astype(jnp.bfloat16)
        down = pair(low, near, rest, 1)
        down_cat[rows, 0:128] = down.astype(jnp.bfloat16)
        down_cat[rows, 128:256] = down.astype(jnp.bfloat16)


def project_kernel(states, out_cat, out):
    levels = states[pl.ds(8, 64, stride=9), :]
    low = low_lanes(64)
    rows = []
    for r in range(8):
        level = jnp.where(low, levels[:, r : r + 1], levels[:, HD + r : HD + r + 1])
        share = jnp.exp(level - jnp.max(level, axis=0, keepdims=True))
        value = jnp.sum(share * states[pl.ds(r, 64, stride=9), :], axis=0, keepdims=True)
        rows.append(value / jnp.sum(share, axis=0, keepdims=True))
    near, rest, _ = parts_of(jnp.concatenate(rows, axis=0))
    near, rest = near.astype(jnp.float32), rest.astype(jnp.float32)
    left = jnp.concatenate(
        [jnp.concatenate([near, near], axis=1), jnp.concatenate([rest, rest], axis=1)], axis=0
    ).astype(jnp.bfloat16)
    both = lax.dot_general(left, out_cat[...], NT, preferred_element_type=jnp.float32)
    partial = both[0:8] + both[8:16]
    for copy in range(8):
        for c in range(8):
            out[copy, pl.ds(c, 8, stride=8), :] = partial[:, c * 128 : (c + 1) * 128]


def latent_kernel(rows, in_cat, down_cat, out):
    row = jnp.concatenate([rows[pl.ds(c, 64, stride=8), :] for c in range(8)], axis=1)
    near, rest, _ = parts_of(normalized(row))
    raw = jnp.dot(
        jnp.concatenate([near, rest], axis=0), in_cat[...], preferred_element_type=jnp.float32
    )
    raw = raw[0:64] + raw[64:128]
    hidden = jax.nn.gelu(raw + pltpu.roll(raw, HD, 1))
    near, rest, _ = parts_of(hidden)
    left = jnp.concatenate([near, rest], axis=1)
    down = lax.dot_general(left, down_cat[...], NT, preferred_element_type=jnp.float32)
    for c in range(8):
        out[pl.ds(c, 64, stride=8), :] = down[:, c * 128 : (c + 1) * 128]


VMEM = pl.BlockSpec(memory_space=pltpu.VMEM)
SMEM = pl.BlockSpec(memory_space=pltpu.SMEM)


def shape(*dims):
    return jax.ShapeDtypeStruct(dims, jnp.float32)


def params(**more):
    return pltpu.CompilerParams(vmem_limit_bytes=56 * 1024 * 1024, **more)


def exchange(value, axes):
    return lax.all_to_all(value, axes, 0, 0)


def per_device(token_ids, token_table, row_table, col_table, chan_table, w_query, w_key, w_value, w_out, w_in, w_down):
    index = lax.axis_index(POS).astype(jnp.int32).reshape(1)

    bf16 = lambda *dims: jax.ShapeDtypeStruct(dims, jnp.bfloat16)
    whole = lambda *dims: pl.BlockSpec(dims, lambda i: (0,) * len(dims))
    slab = lambda *dims: pl.BlockSpec(dims, lambda i: (i,) + (0,) * (len(dims) - 1))
    lanes = lambda *dims: pl.BlockSpec(dims, lambda i: (0, i))
    middle = lambda *dims: pl.BlockSpec(dims, lambda i: (0, i, 0))

    with jax.named_scope("weights"):
        packed = pl.pallas_call(
            pack_kernel,
            in_specs=[VMEM] * 4,
            out_specs=VMEM,
            out_shape=shape(8, 40, 128),
            compiler_params=params(),
            name="pack",
        )(token_ids.reshape(8, 128), w_out.T, w_in, w_down.T)
        packed = exchange(packed, "z")

    width = 256
    tables = pl.pallas_call(
        tables_kernel,
        grid=(D // width,),
        in_specs=[lanes(VOCAB, width), lanes(ROWS_USED, width), lanes(IMG, width), lanes(3, width)],
        out_specs=[lanes(VOCAB, width)] * 3 + [lanes(384, width)] * 3 + [lanes(LAT, width)],
        out_shape=[bf16(VOCAB, D)] * 3 + [bf16(384, D)] * 3 + [shape(LAT, D)],
        compiler_params=params(),
        cost_estimate=pl.CostEstimate(flops=2 * 10**9, transcendentals=0, bytes_accessed=8 * 10**6),
        name="tables",
    )(token_table, row_table, col_table, chan_table)
    packed, tables = lax.optimization_barrier((packed, tables))
    *splits, where_sum = tables
    tokens = splits[:3]

    with jax.named_scope("columns"):
        packed = jnp.concatenate([packed[:, :32, :].reshape(256, 128), packed[7, 32:, :]], axis=0)
        weights = exchange(jnp.broadcast_to(packed[None], (8, 264, 128)), COLUMN)

    block = POS_DEV // KEY_STEPS
    key_cat, value_cat = pl.pallas_call(
        keys_kernel,
        grid=(KEY_STEPS,),
        in_specs=[SMEM, whole(8, 128)] + [whole(VOCAB, D)] * 3 + [whole(384, D)] * 3 + [whole(D, 128)] * 2,
        out_specs=[middle(2, block, 384), middle(2, block, 256)],
        out_shape=[bf16(2, POS_DEV, 384), bf16(2, POS_DEV, 256)],
        compiler_params=params(),
        cost_estimate=pl.CostEstimate(flops=8 * 10**9, transcendentals=0, bytes_accessed=10**7),
        name="keys",
    )(index, token_ids.reshape(8, 128), *splits, w_key, w_value)

    size = LAT // LATENT_STEPS
    states = pl.pallas_call(
        attend_kernel,
        grid=(LATENT_STEPS,),
        in_specs=[SMEM, whole(8, 128), slab(size, D)]
        + [whole(VOCAB, D)] * 3
        + [whole(D, 128), whole(2, POS_DEV, 384), whole(2, POS_DEV, 256)],
        out_specs=slab(size // 8 * 9, 128),
        out_shape=shape(64 * 9, 128),
        scratch_shapes=[pltpu.VMEM((size, 128), jnp.float32)],
        compiler_params=params(),
        cost_estimate=pl.CostEstimate(flops=6 * 10**9, transcendentals=10**6, bytes_accessed=10**7),
        name="attend",
    )(index, weights[7, 256:264, :], where_sum, *tokens, w_query, key_cat, value_cat)

    with jax.named_scope("states"):
        states = exchange(states.reshape(64, 1, 1152), POS).reshape(64 * 9, 128)
    out_cat, in_cat, down_cat = pl.pallas_call(
        prepare_kernel,
        in_specs=[VMEM],
        out_specs=[VMEM] * 3,
        out_shape=[bf16(D, 256), bf16(D, 128), bf16(D, 256)],
        compiler_params=params(),
        cost_estimate=pl.CostEstimate(flops=10**9, transcendentals=0, bytes_accessed=3 * 10**6),
        name="prepare",
    )(weights)
    partial_rows = pl.pallas_call(
        project_kernel,
        in_specs=[VMEM, VMEM],
        out_specs=VMEM,
        out_shape=shape(8, 64, 128),
        compiler_params=params(),
        name="project",
    )(states, out_cat)
    with jax.named_scope("projected"):
        projected = jnp.sum(exchange(partial_rows, HEAD), axis=0)
        rows = exchange(jnp.broadcast_to(projected[None], (8, 64, 128)), "z")
    outs = pl.pallas_call(
        latent_kernel,
        in_specs=[VMEM] * 3,
        out_specs=VMEM,
        out_shape=shape(512, 128),
        compiler_params=params(),
        name="latent",
    )(rows.reshape(512, 128), in_cat, down_cat)
    with jax.named_scope("result"):
        own = jnp.sum(exchange(outs.reshape(8, 64, 128), "z"), axis=0)
        total = jnp.sum(exchange(jnp.broadcast_to(own[None], (8, 64, 128)), HEAD), axis=0)
        return (projected + total).reshape(8, D)


def solution(mesh):
    fine = Mesh(mesh.devices.reshape(8, 2, 4, 4, 2), ("z", "ylo", "x", "yhi", "core"))
    placed = (
        P(POS),
        P(),
        P(),
        P(),
        P(),
        P(None, HEAD),
        P(None, HEAD),
        P(None, HEAD),
        P(HEAD, POS),
        P(POS, HEAD),
        P(HEAD, POS),
    )
    return jax.shard_map(
        per_device, mesh=fine, in_specs=placed, out_specs=P(POS, None), check_vma=False
    )
```

```python
import jax
import jax.numpy as jnp
from jax import lax
from jax.experimental import pallas as pl
from jax.experimental.pallas import tpu as pltpu
from jax.sharding import Mesh
from jax.sharding import PartitionSpec as P

D = 1024
HD = 64
IMG = 256
LAT = 512
POS_DEV = 1024
POSITIONS = 65536
VOCAB = 256
ROWS_USED = 88
KEY_STEPS = 1
LATENT_STEPS = 1
KEY_PARTS = 2
QUERY_PARTS = 2

POS = ("z", "ylo", "x")
HEAD = ("yhi", "core")
COLUMN = ("ylo", "x")

HIGHEST = lax.Precision.HIGHEST
NT = (((1,), (1,)), ((), ()))
NN = (((1,), (0,)), ((), ()))


def parts_of(values):
    parts = []
    for _ in range(3):
        rounded = values.astype(jnp.bfloat16)
        parts.append(rounded)
        values = values - rounded.astype(jnp.float32)
    return parts


def store_parts(refs, at, values):
    for ref, part in zip(refs, parts_of(values)):
        ref[pl.ds(at, values.shape[0]), :] = part


def place(first, rows):
    base = first // 3
    step = lax.broadcasted_iota(jnp.int32, (rows, 1), 0) + (first - base * 3)
    third = (step * 21846) >> 16
    return step - third * 3, base + third


def hot(mask):
    return jnp.where(mask, 1.0, 0.0).astype(jnp.bfloat16)


def hot_place(first, rows):
    channel, pixel = place(first, rows)
    lane = lax.broadcasted_iota(jnp.int32, (rows, 256), 1)
    tail = lax.broadcasted_iota(jnp.int32, (rows, 128), 1)
    in_tail = (tail == (pixel >> 8)) | (tail == channel + ROWS_USED)
    return jnp.concatenate([hot(lane == (pixel & 255)), hot(in_tail)], axis=1)


def id_columns(ids, size, skip):
    turned = jnp.transpose(ids)
    column = lax.broadcasted_iota(jnp.int32, turned.shape, 1)
    start = skip + pl.program_id(0) * (size // 128)
    picked = [
        jnp.sum(jnp.where(column == start + i, turned, 0.0), axis=1, keepdims=True)
        for i in range(size // 128)
    ]
    return jnp.concatenate(picked, axis=0).astype(jnp.int32)


def hot_token(ids):
    return hot(lax.broadcasted_iota(jnp.int32, (ids.shape[0], VOCAB), 1) == ids)


def pick(picks, parts):
    total = None
    for part in reversed(parts):
        piece = lax.dot_general(picks, part, NN, preferred_element_type=jnp.float32)
        total = piece if total is None else total + piece
    return total


def normalized(total):
    center = total - jnp.mean(total, axis=-1, keepdims=True)
    spread = jnp.mean(center * center, axis=-1, keepdims=True)
    return center * lax.rsqrt(spread + 1e-05)


def low_lanes(rows):
    return lax.broadcasted_iota(jnp.int32, (rows, 2 * HD), 1) < HD


def pair(low, first, second, head):
    if head == 0:
        return jnp.where(low, first, pltpu.roll(second, HD, 1))
    return jnp.where(low, pltpu.roll(first, HD, 1), second)


def pack_kernel(ids, w_out, w_in, w_down, packed):
    low = low_lanes(16)
    own_ids = ids[...].astype(jnp.float32)
    for b in range(8):
        lanes = slice(b // 2 * 128, b // 2 * 128 + 128)
        packed[b, 0:16, :] = w_out[...]
        packed[b, 16:32, :] = pair(low, w_in[:, lanes], w_down[:, lanes], b % 2)
        packed[b, 32:40, :] = own_ids


def tables_kernel(token, row, col, chan, t1, t2, t3, p1, p2, p3, where_sum):
    tokens, places = (t1, t2, t3), (p1, p2, p3)
    for at in (0, 128):
        store_parts(tokens, at, token[pl.ds(at, 128), :])
        store_parts(places, at, col[pl.ds(at, 128), :])
    rest = jnp.zeros((128 - ROWS_USED - 3, token.shape[1]), jnp.float32)
    store_parts(places, 256, jnp.concatenate([row[...], chan[...], rest], axis=0))
    where_sum[...] = pick(hot_place(POSITIONS - LAT, LAT), [p[...] for p in places])


def keys_kernel(index, ids, t1, t2, t3, p1, p2, p3, w_key, w_value, key_cat, value_cat):
    size = POS_DEV // KEY_STEPS
    part_size = size // KEY_PARTS
    first = index[0] * POS_DEV + pl.program_id(0) * size
    columns = id_columns(ids[...].astype(jnp.float32), size, 0)
    places = [p1[...], p2[...], p3[...]]
    tokens = [t1[...], t2[...], t3[...]]
    embs = []
    for i in range(KEY_PARTS):
        total = pick(hot_place(first + i * part_size, part_size), places)
        total = total + pick(hot_token(columns[i * part_size : (i + 1) * part_size]), tokens)
        embs.append(normalized(total))
    wide = jnp.concatenate([w_key[...], w_value[...]], axis=1)
    both = jnp.concatenate([jnp.dot(emb, wide, precision=HIGHEST) for emb in embs], axis=0)
    keys, values = both[:, :128], both[:, 128:]
    low = low_lanes(size)
    k = [part.astype(jnp.float32) for part in parts_of(keys)]
    v = [part.astype(jnp.float32) for part in parts_of(values)]
    ones = jnp.ones_like(values)
    for head in range(2):
        both = pair(low, k[0], k[1], head)
        pieces = [pair(low, k[2], k[0], head), both, pair(low, k[2], k[1], head)]
        for i, piece in enumerate(pieces):
            key_cat[head, :, i * 128 : (i + 1) * 128] = piece.astype(jnp.bfloat16)
        tail = jnp.where(low, v[2], ones) if head == 0 else jnp.where(low, ones, v[2])
        value_cat[head, :, 0:128] = pair(low, v[0], v[1], head).astype(jnp.bfloat16)
        value_cat[head, :, 128:256] = tail.astype(jnp.bfloat16)


def attend_kernel(index, ids, where_sum, t1, t2, t3, w_query, key_cat, value_cat, out, attended):
    block = pl.program_id(0)
    size = where_sum.shape[0]
    columns = id_columns(ids[...], size, (POS_DEV - LAT) // 128)
    tokens = [t1[...], t2[...], t3[...]]
    w = parts_of(w_query[...])
    near_w = jnp.concatenate([w[0], w[1]], axis=1)
    far_w = jnp.concatenate([w[2], w[0]], axis=0)
    part_size = size // QUERY_PARTS
    low = low_lanes(part_size)
    parts = [slice(i * part_size, (i + 1) * part_size) for i in range(QUERY_PARTS)]
    all_q = []
    for rows in parts:
        e = parts_of(normalized(where_sum[rows] + pick(hot_token(columns[rows]), tokens)))
        wide = jnp.dot(e[0], near_w, preferred_element_type=jnp.float32)
        wide = wide + jnp.dot(e[1], near_w, preferred_element_type=jnp.float32)
        wide = wide[:, :128] + wide[:, 128:]
        wide = wide + jnp.dot(
            jnp.concatenate([e[0], e[2]], axis=1), far_w, preferred_element_type=jnp.float32
        )
        all_q.append([part.astype(jnp.float32) for part in parts_of(wide * HD ** (-0.5))])
    levels = []
    for rows, q in zip(parts, all_q):
        late = POS_DEV - LAT
        where = lax.broadcasted_iota(jnp.int32, (part_size, LAT), 1) + (index[0] * POS_DEV + late)
        latent = lax.broadcasted_iota(jnp.int32, (part_size, LAT), 0)
        seen = where <= latent + (POSITIONS - LAT + block * size + rows.start)
        sums, weights, tops = [], [], []
        for head in range(2):
            key = key_cat[head]
            lead = jnp.concatenate([pair(low, q[0], q[2], head), pair(low, q[0], q[0], head)], axis=1)
            rest = jnp.concatenate([pair(low, q[1], q[1], head), pair(low, q[1], q[2], head)], axis=1)
            scores = lax.dot_general(
                lead.astype(jnp.bfloat16), key[:, 0:256], NT, preferred_element_type=jnp.float32
            ) + lax.dot_general(
                rest.astype(jnp.bfloat16), key[:, 128:384], NT, preferred_element_type=jnp.float32
            )
            scores = jnp.concatenate(
                [scores[:, :late], jnp.where(seen, scores[:, late:], -1e30)], axis=1
            )
            top = jnp.max(scores, axis=-1, keepdims=True)
            probs = jnp.exp(scores - top)
            near = probs.astype(jnp.bfloat16)
            rest = (probs - near.astype(jnp.float32)).astype(jnp.bfloat16)
            value = value_cat[head]
            both = jnp.dot(near, value, preferred_element_type=jnp.float32)
            both = both + jnp.dot(rest, value, preferred_element_type=jnp.float32)
            lead, tail = both[:, :128], both[:, 128:]
            sums.append(lead + pltpu.roll(lead, HD, 1) + tail)
            weights.append(pltpu.roll(tail, HD, 1))
            tops.append(top)
        weight = jnp.where(low, weights[0], weights[1])
        levels.append(jnp.where(low, tops[0], tops[1]) + jnp.log(weight))
        attended[rows] = jnp.where(low, sums[0], sums[1]) / weight
    level = jnp.concatenate(levels, axis=0)
    chunks = size // 8
    for r in range(8):
        out[pl.ds(r, chunks, stride=9), :] = attended[pl.ds(r, chunks, stride=8), :]
    level = level.reshape(chunks, 8, 128)
    lane = lax.broadcasted_iota(jnp.int32, level.shape, 2)
    lat = lax.broadcasted_iota(jnp.int32, level.shape, 1)
    out[pl.ds(8, chunks, stride=9), :] = jnp.sum(jnp.where((lane & 7) == lat, level, 0.0), axis=1)


def prepare_kernel(weights, out_cat, in_cat, down_cat):
    for c in range(8):
        rows = pl.ds(c * 128, 128)
        near, rest, _ = parts_of(weights[:, c * 32 : c * 32 + 16, :].reshape(128, 128))
        out_cat[rows, 0:128] = near
        out_cat[rows, 128:256] = rest
        near, rest, _ = parts_of(weights[:, c * 32 + 16 : c * 32 + 32, :].reshape(128, 128))
        near, rest = near.astype(jnp.float32), rest.astype(jnp.float32)
        low = low_lanes(128)
        in_cat[rows, :] = pair(low, near, rest, 0).astype(jnp.bfloat16)
        down = pair(low, near, rest, 1)
        down_cat[rows, 0:128] = down.astype(jnp.bfloat16)
        down_cat[rows, 128:256] = down.astype(jnp.bfloat16)


def project_kernel(states, out_cat, out):
    levels = states[pl.ds(8, 64, stride=9), :]
    low = low_lanes(64)
    rows = []
    for r in range(8):
        level = jnp.where(low, levels[:, r : r + 1], levels[:, HD + r : HD + r + 1])
        share = jnp.exp(level - jnp.max(level, axis=0, keepdims=True))
        value = jnp.sum(share * states[pl.ds(r, 64, stride=9), :], axis=0, keepdims=True)
        rows.append(value / jnp.sum(share, axis=0, keepdims=True))
    near, rest, _ = parts_of(jnp.concatenate(rows, axis=0))
    near, rest = near.astype(jnp.float32), rest.astype(jnp.float32)
    left = jnp.concatenate(
        [jnp.concatenate([near, near], axis=1), jnp.concatenate([rest, rest], axis=1)], axis=0
    ).astype(jnp.bfloat16)
    both = lax.dot_general(left, out_cat[...], NT, preferred_element_type=jnp.float32)
    partial = both[0:8] + both[8:16]
    for copy in range(8):
        for c in range(8):
            out[copy, pl.ds(c, 8, stride=8), :] = partial[:, c * 128 : (c + 1) * 128]


def latent_kernel(rows, in_cat, down_cat, out):
    row = jnp.concatenate([rows[pl.ds(c, 64, stride=8), :] for c in range(8)], axis=1)
    near, rest, _ = parts_of(normalized(row))
    raw = jnp.dot(
        jnp.concatenate([near, rest], axis=0), in_cat[...], preferred_element_type=jnp.float32
    )
    raw = raw[0:64] + raw[64:128]
    hidden = jax.nn.gelu(raw + pltpu.roll(raw, HD, 1))
    near, rest, _ = parts_of(hidden)
    left = jnp.concatenate([near, rest], axis=1)
    down = lax.dot_general(left, down_cat[...], NT, preferred_element_type=jnp.float32)
    for c in range(8):
        out[pl.ds(c, 64, stride=8), :] = down[:, c * 128 : (c + 1) * 128]


VMEM = pl.BlockSpec(memory_space=pltpu.VMEM)
SMEM = pl.BlockSpec(memory_space=pltpu.SMEM)


def shape(*dims):
    return jax.ShapeDtypeStruct(dims, jnp.float32)


def params(**more):
    return pltpu.CompilerParams(vmem_limit_bytes=56 * 1024 * 1024, **more)


def near(value):
    return pltpu.with_memory_space_constraint(value, pltpu.VMEM)


def exchange(value, axes):
    return lax.all_to_all(value, axes, 0, 0)


def per_device(token_ids, token_table, row_table, col_table, chan_table, w_query, w_key, w_value, w_out, w_in, w_down):
    index = lax.axis_index(POS).astype(jnp.int32).reshape(1)

    bf16 = lambda *dims: jax.ShapeDtypeStruct(dims, jnp.bfloat16)
    whole = lambda *dims: pl.BlockSpec(dims, lambda i: (0,) * len(dims))
    slab = lambda *dims: pl.BlockSpec(dims, lambda i: (i,) + (0,) * (len(dims) - 1))
    lanes = lambda *dims: pl.BlockSpec(dims, lambda i: (0, i))
    middle = lambda *dims: pl.BlockSpec(dims, lambda i: (0, i, 0))

    with jax.named_scope("weights"):
        packed = pl.pallas_call(
            pack_kernel,
            in_specs=[VMEM] * 4,
            out_specs=VMEM,
            out_shape=shape(8, 40, 128),
            compiler_params=params(),
            name="pack",
        )(token_ids.reshape(8, 128), w_out.T, w_in, w_down.T)
        packed = exchange(packed, "z")

    width = 256
    tables = pl.pallas_call(
        tables_kernel,
        grid=(D // width,),
        in_specs=[lanes(VOCAB, width), lanes(ROWS_USED, width), lanes(IMG, width), lanes(3, width)],
        out_specs=[lanes(VOCAB, width)] * 3 + [lanes(384, width)] * 3 + [lanes(LAT, width)],
        out_shape=[bf16(VOCAB, D)] * 3 + [bf16(384, D)] * 3 + [shape(LAT, D)],
        compiler_params=params(),
        cost_estimate=pl.CostEstimate(flops=2 * 10**9, transcendentals=0, bytes_accessed=8 * 10**6),
        name="tables",
    )(token_table, row_table, col_table, chan_table)
    packed, tables = lax.optimization_barrier((packed, tables))
    *splits, where_sum = tables
    tokens = splits[:3]

    with jax.named_scope("columns"):
        packed = jnp.concatenate([packed[:, :32, :].reshape(256, 128), packed[7, 32:, :]], axis=0)
        weights = exchange(jnp.broadcast_to(packed[None], (8, 264, 128)), COLUMN)

    block = POS_DEV // KEY_STEPS
    key_cat, value_cat = pl.pallas_call(
        keys_kernel,
        grid=(KEY_STEPS,),
        in_specs=[SMEM, whole(8, 128)] + [whole(VOCAB, D)] * 3 + [whole(384, D)] * 3 + [whole(D, 128)] * 2,
        out_specs=[middle(2, block, 384), middle(2, block, 256)],
        out_shape=[bf16(2, POS_DEV, 384), bf16(2, POS_DEV, 256)],
        compiler_params=params(),
        cost_estimate=pl.CostEstimate(flops=8 * 10**9, transcendentals=0, bytes_accessed=10**7),
        name="keys",
    )(index, token_ids.reshape(8, 128), *splits, w_key, w_value)

    size = LAT // LATENT_STEPS
    states = pl.pallas_call(
        attend_kernel,
        grid=(LATENT_STEPS,),
        in_specs=[SMEM, whole(8, 128), slab(size, D)]
        + [whole(VOCAB, D)] * 3
        + [whole(D, 128), whole(2, POS_DEV, 384), whole(2, POS_DEV, 256)],
        out_specs=slab(size // 8 * 9, 128),
        out_shape=shape(64 * 9, 128),
        scratch_shapes=[pltpu.VMEM((size, 128), jnp.float32)],
        compiler_params=params(),
        cost_estimate=pl.CostEstimate(flops=6 * 10**9, transcendentals=10**6, bytes_accessed=10**7),
        name="attend",
    )(index, weights[7, 256:264, :], where_sum, *tokens, w_query, key_cat, value_cat)

    with jax.named_scope("states"):
        states = exchange(states.reshape(64, 1, 1152), POS).reshape(64 * 9, 128)
    out_cat, in_cat, down_cat = pl.pallas_call(
        prepare_kernel,
        in_specs=[VMEM],
        out_specs=[VMEM] * 3,
        out_shape=[bf16(D, 256), bf16(D, 128), bf16(D, 256)],
        compiler_params=params(),
        cost_estimate=pl.CostEstimate(flops=10**9, transcendentals=0, bytes_accessed=3 * 10**6),
        name="prepare",
    )(weights)
    partial_rows = pl.pallas_call(
        project_kernel,
        in_specs=[VMEM, VMEM],
        out_specs=VMEM,
        out_shape=shape(8, 64, 128),
        compiler_params=params(),
        name="project",
    )(near(states), near(out_cat))
    with jax.named_scope("projected"):
        projected = jnp.sum(exchange(partial_rows, HEAD), axis=0)
        rows = exchange(jnp.broadcast_to(projected[None], (8, 64, 128)), "z")
    outs = pl.pallas_call(
        latent_kernel,
        in_specs=[VMEM] * 3,
        out_specs=VMEM,
        out_shape=shape(512, 128),
        compiler_params=params(),
        name="latent",
    )(near(rows.reshape(512, 128)), near(in_cat), near(down_cat))
    with jax.named_scope("result"):
        own = jnp.sum(exchange(outs.reshape(8, 64, 128), "z"), axis=0)
        total = jnp.sum(exchange(jnp.broadcast_to(own[None], (8, 64, 128)), HEAD), axis=0)
        return (projected + total).reshape(8, D)


def solution(mesh):
    fine = Mesh(mesh.devices.reshape(8, 2, 4, 4, 2), ("z", "ylo", "x", "yhi", "core"))
    placed = (
        P(POS),
        P(),
        P(),
        P(),
        P(),
        P(None, HEAD),
        P(None, HEAD),
        P(None, HEAD),
        P(HEAD, POS),
        P(POS, HEAD),
        P(HEAD, POS),
    )
    return jax.shard_map(
        per_device, mesh=fine, in_specs=placed, out_specs=P(POS, None), check_vma=False
    )
```

```python
import jax
import jax.numpy as jnp
from jax import lax
from jax.experimental import pallas as pl
from jax.experimental.pallas import tpu as pltpu
from jax.sharding import Mesh
from jax.sharding import PartitionSpec as P

D = 1024
HD = 64
IMG = 256
LAT = 512
POS_DEV = 1024
POSITIONS = 65536
VOCAB = 256
ROWS_USED = 88
KEY_STEPS = 1
LATENT_STEPS = 1
KEY_PARTS = 2
QUERY_PARTS = 2

POS = ("z", "ylo", "x")
HEAD = ("yhi", "core")
COLUMN = ("ylo", "x")

HIGHEST = lax.Precision.HIGHEST
NT = (((1,), (1,)), ((), ()))
NN = (((1,), (0,)), ((), ()))


def parts_of(values):
    parts = []
    for _ in range(3):
        rounded = values.astype(jnp.bfloat16)
        parts.append(rounded)
        values = values - rounded.astype(jnp.float32)
    return parts


def store_parts(refs, at, values):
    for ref, part in zip(refs, parts_of(values)):
        ref[pl.ds(at, values.shape[0]), :] = part


def place(first, rows):
    base = first // 3
    step = lax.broadcasted_iota(jnp.int32, (rows, 1), 0) + (first - base * 3)
    third = (step * 21846) >> 16
    return step - third * 3, base + third


def hot(mask):
    return jnp.where(mask, 1.0, 0.0).astype(jnp.bfloat16)


def hot_place(first, rows):
    channel, pixel = place(first, rows)
    lane = lax.broadcasted_iota(jnp.int32, (rows, 256), 1)
    tail = lax.broadcasted_iota(jnp.int32, (rows, 128), 1)
    in_tail = (tail == (pixel >> 8)) | (tail == channel + ROWS_USED)
    return jnp.concatenate([hot(lane == (pixel & 255)), hot(in_tail)], axis=1)


def id_columns(ids, size, skip):
    turned = jnp.transpose(ids)
    column = lax.broadcasted_iota(jnp.int32, turned.shape, 1)
    start = skip + pl.program_id(0) * (size // 128)
    picked = [
        jnp.sum(jnp.where(column == start + i, turned, 0.0), axis=1, keepdims=True)
        for i in range(size // 128)
    ]
    return jnp.concatenate(picked, axis=0).astype(jnp.int32)


def hot_token(ids):
    return hot(lax.broadcasted_iota(jnp.int32, (ids.shape[0], VOCAB), 1) == ids)


def pick(picks, parts):
    total = None
    for part in reversed(parts):
        piece = lax.dot_general(picks, part, NN, preferred_element_type=jnp.float32)
        total = piece if total is None else total + piece
    return total


def normalized(total):
    center = total - jnp.mean(total, axis=-1, keepdims=True)
    spread = jnp.mean(center * center, axis=-1, keepdims=True)
    return center * lax.rsqrt(spread + 1e-05)


def low_lanes(rows):
    return lax.broadcasted_iota(jnp.int32, (rows, 2 * HD), 1) < HD


def pair(low, first, second, head):
    if head == 0:
        return jnp.where(low, first, pltpu.roll(second, HD, 1))
    return jnp.where(low, pltpu.roll(first, HD, 1), second)


def pack_kernel(ids, w_out, w_in, w_down, packed):
    low = low_lanes(16)
    own_ids = ids[...].astype(jnp.float32)
    for b in range(8):
        lanes = slice(b // 2 * 128, b // 2 * 128 + 128)
        packed[b, 0:16, :] = w_out[...]
        packed[b, 16:32, :] = pair(low, w_in[:, lanes], w_down[:, lanes], b % 2)
        packed[b, 32:40, :] = own_ids


def tables_kernel(token, row, col, chan, t1, t2, t3, p1, p2, p3, where_sum):
    tokens, places = (t1, t2, t3), (p1, p2, p3)
    for at in (0, 128):
        store_parts(tokens, at, token[pl.ds(at, 128), :])
        store_parts(places, at, col[pl.ds(at, 128), :])
    rest = jnp.zeros((128 - ROWS_USED - 3, token.shape[1]), jnp.float32)
    store_parts(places, 256, jnp.concatenate([row[...], chan[...], rest], axis=0))
    where_sum[...] = pick(hot_place(POSITIONS - LAT, LAT), [p[...] for p in places])


def keys_kernel(index, ids, t1, t2, t3, p1, p2, p3, w_key, w_value, key_cat, value_cat):
    size = POS_DEV // KEY_STEPS
    part_size = size // KEY_PARTS
    first = index[0] * POS_DEV + pl.program_id(0) * size
    columns = id_columns(ids[...].astype(jnp.float32), size, 0)
    places = [p1[...], p2[...], p3[...]]
    tokens = [t1[...], t2[...], t3[...]]
    embs = []
    for i in range(KEY_PARTS):
        total = pick(hot_place(first + i * part_size, part_size), places)
        total = total + pick(hot_token(columns[i * part_size : (i + 1) * part_size]), tokens)
        embs.append(normalized(total))
    wide = jnp.concatenate([w_key[...], w_value[...]], axis=1)
    both = jnp.concatenate([jnp.dot(emb, wide, precision=HIGHEST) for emb in embs], axis=0)
    keys, values = both[:, :128], both[:, 128:]
    low = low_lanes(size)
    k = [part.astype(jnp.float32) for part in parts_of(keys)]
    v = [part.astype(jnp.float32) for part in parts_of(values)]
    ones = jnp.ones_like(values)
    for head in range(2):
        both = pair(low, k[0], k[1], head)
        pieces = [pair(low, k[2], k[0], head), both, pair(low, k[2], k[1], head)]
        for i, piece in enumerate(pieces):
            key_cat[head, :, i * 128 : (i + 1) * 128] = piece.astype(jnp.bfloat16)
        tail = jnp.where(low, v[2], ones) if head == 0 else jnp.where(low, ones, v[2])
        value_cat[head, :, 0:128] = pair(low, v[0], v[1], head).astype(jnp.bfloat16)
        value_cat[head, :, 128:256] = tail.astype(jnp.bfloat16)


def attend_kernel(index, ids, where_sum, t1, t2, t3, w_query, key_cat, value_cat, out, attended):
    block = pl.program_id(0)
    size = where_sum.shape[0]
    columns = id_columns(ids[...], size, (POS_DEV - LAT) // 128)
    tokens = [t1[...], t2[...], t3[...]]
    w = parts_of(w_query[...])
    near_w = jnp.concatenate([w[0], w[1]], axis=1)
    far_w = jnp.concatenate([w[2], w[0]], axis=0)
    part_size = size // QUERY_PARTS
    low = low_lanes(part_size)
    parts = [slice(i * part_size, (i + 1) * part_size) for i in range(QUERY_PARTS)]
    all_q = []
    for rows in parts:
        e = parts_of(normalized(where_sum[rows] + pick(hot_token(columns[rows]), tokens)))
        wide = jnp.dot(e[0], near_w, preferred_element_type=jnp.float32)
        wide = wide + jnp.dot(e[1], near_w, preferred_element_type=jnp.float32)
        wide = wide[:, :128] + wide[:, 128:]
        wide = wide + jnp.dot(
            jnp.concatenate([e[0], e[2]], axis=1), far_w, preferred_element_type=jnp.float32
        )
        all_q.append([part.astype(jnp.float32) for part in parts_of(wide * HD ** (-0.5))])
    levels = []
    for rows, q in zip(parts, all_q):
        late = POS_DEV - LAT
        where = lax.broadcasted_iota(jnp.int32, (part_size, LAT), 1) + (index[0] * POS_DEV + late)
        latent = lax.broadcasted_iota(jnp.int32, (part_size, LAT), 0)
        seen = where <= latent + (POSITIONS - LAT + block * size + rows.start)
        sums, weights, tops = [], [], []
        for head in range(2):
            key = key_cat[head]
            lead = jnp.concatenate([pair(low, q[0], q[2], head), pair(low, q[0], q[0], head)], axis=1)
            rest = jnp.concatenate([pair(low, q[1], q[1], head), pair(low, q[1], q[2], head)], axis=1)
            scores = lax.dot_general(
                lead.astype(jnp.bfloat16), key[:, 0:256], NT, preferred_element_type=jnp.float32
            ) + lax.dot_general(
                rest.astype(jnp.bfloat16), key[:, 128:384], NT, preferred_element_type=jnp.float32
            )
            scores = jnp.concatenate(
                [scores[:, :late], jnp.where(seen, scores[:, late:], -1e30)], axis=1
            )
            top = jnp.max(scores, axis=-1, keepdims=True)
            probs = jnp.exp(scores - top)
            near = probs.astype(jnp.bfloat16)
            rest = (probs - near.astype(jnp.float32)).astype(jnp.bfloat16)
            value = value_cat[head]
            both = jnp.dot(near, value, preferred_element_type=jnp.float32)
            both = both + jnp.dot(rest, value, preferred_element_type=jnp.float32)
            lead, tail = both[:, :128], both[:, 128:]
            sums.append(lead + pltpu.roll(lead, HD, 1) + tail)
            weights.append(pltpu.roll(tail, HD, 1))
            tops.append(top)
        weight = jnp.where(low, weights[0], weights[1])
        levels.append(jnp.where(low, tops[0], tops[1]) + jnp.log(weight))
        attended[rows] = jnp.where(low, sums[0], sums[1]) / weight
    level = jnp.concatenate(levels, axis=0)
    chunks = size // 8
    for r in range(8):
        out[pl.ds(r, chunks, stride=9), :] = attended[pl.ds(r, chunks, stride=8), :]
    level = level.reshape(chunks, 8, 128)
    lane = lax.broadcasted_iota(jnp.int32, level.shape, 2)
    lat = lax.broadcasted_iota(jnp.int32, level.shape, 1)
    out[pl.ds(8, chunks, stride=9), :] = jnp.sum(jnp.where((lane & 7) == lat, level, 0.0), axis=1)


def prepare_kernel(weights, out_cat, in_cat, down_cat):
    for c in range(8):
        rows = pl.ds(c * 128, 128)
        near, rest, _ = parts_of(weights[:, c * 32 : c * 32 + 16, :].reshape(128, 128))
        out_cat[rows, 0:128] = near
        out_cat[rows, 128:256] = rest
        near, rest, _ = parts_of(weights[:, c * 32 + 16 : c * 32 + 32, :].reshape(128, 128))
        near, rest = near.astype(jnp.float32), rest.astype(jnp.float32)
        low = low_lanes(128)
        in_cat[rows, :] = pair(low, near, rest, 0).astype(jnp.bfloat16)
        down = pair(low, near, rest, 1)
        down_cat[rows, 0:128] = down.astype(jnp.bfloat16)
        down_cat[rows, 128:256] = down.astype(jnp.bfloat16)


def project_kernel(states, out_cat, out):
    levels = states[pl.ds(8, 64, stride=9), :]
    low = low_lanes(64)
    rows = []
    for r in range(8):
        level = jnp.where(low, levels[:, r : r + 1], levels[:, HD + r : HD + r + 1])
        share = jnp.exp(level - jnp.max(level, axis=0, keepdims=True))
        value = jnp.sum(share * states[pl.ds(r, 64, stride=9), :], axis=0, keepdims=True)
        rows.append(value / jnp.sum(share, axis=0, keepdims=True))
    near, rest, _ = parts_of(jnp.concatenate(rows, axis=0))
    near, rest = near.astype(jnp.float32), rest.astype(jnp.float32)
    left = jnp.concatenate(
        [jnp.concatenate([near, near], axis=1), jnp.concatenate([rest, rest], axis=1)], axis=0
    ).astype(jnp.bfloat16)
    both = lax.dot_general(left, out_cat[...], NT, preferred_element_type=jnp.float32)
    partial = both[0:8] + both[8:16]
    for copy in range(8):
        for c in range(8):
            out[copy, pl.ds(c, 8, stride=8), :] = partial[:, c * 128 : (c + 1) * 128]


def latent_kernel(rows, in_cat, down_cat, out):
    row = jnp.concatenate([rows[pl.ds(c, 64, stride=8), :] for c in range(8)], axis=1)
    near, rest, _ = parts_of(normalized(row))
    raw = jnp.dot(
        jnp.concatenate([near, rest], axis=0), in_cat[...], preferred_element_type=jnp.float32
    )
    raw = raw[0:64] + raw[64:128]
    hidden = jax.nn.gelu(raw + pltpu.roll(raw, HD, 1))
    near, rest, _ = parts_of(hidden)
    left = jnp.concatenate([near, rest], axis=1)
    down = lax.dot_general(left, down_cat[...], NT, preferred_element_type=jnp.float32)
    for c in range(8):
        out[pl.ds(c, 64, stride=8), :] = down[:, c * 128 : (c + 1) * 128]


VMEM = pl.BlockSpec(memory_space=pltpu.VMEM)
SMEM = pl.BlockSpec(memory_space=pltpu.SMEM)


def shape(*dims):
    return jax.ShapeDtypeStruct(dims, jnp.float32)


def params(**more):
    return pltpu.CompilerParams(vmem_limit_bytes=56 * 1024 * 1024, **more)


def near(value):
    return pltpu.with_memory_space_constraint(value, pltpu.VMEM)


def exchange(value, axes):
    return lax.all_to_all(value, axes, 0, 0)


def per_device(token_ids, token_table, row_table, col_table, chan_table, w_query, w_key, w_value, w_out, w_in, w_down):
    index = lax.axis_index(POS).astype(jnp.int32).reshape(1)

    bf16 = lambda *dims: jax.ShapeDtypeStruct(dims, jnp.bfloat16)
    whole = lambda *dims: pl.BlockSpec(dims, lambda i: (0,) * len(dims))
    slab = lambda *dims: pl.BlockSpec(dims, lambda i: (i,) + (0,) * (len(dims) - 1))
    lanes = lambda *dims: pl.BlockSpec(dims, lambda i: (0, i))
    middle = lambda *dims: pl.BlockSpec(dims, lambda i: (0, i, 0))

    with jax.named_scope("weights"):
        packed = pl.pallas_call(
            pack_kernel,
            in_specs=[VMEM] * 4,
            out_specs=VMEM,
            out_shape=shape(8, 40, 128),
            compiler_params=params(),
            name="pack",
        )(token_ids.reshape(8, 128), w_out.T, w_in, w_down.T)
        packed = exchange(packed, "z")

    width = 256
    tables = pl.pallas_call(
        tables_kernel,
        grid=(D // width,),
        in_specs=[lanes(VOCAB, width), lanes(ROWS_USED, width), lanes(IMG, width), lanes(3, width)],
        out_specs=[lanes(VOCAB, width)] * 3 + [lanes(384, width)] * 3 + [lanes(LAT, width)],
        out_shape=[bf16(VOCAB, D)] * 3 + [bf16(384, D)] * 3 + [shape(LAT, D)],
        compiler_params=params(),
        cost_estimate=pl.CostEstimate(flops=2 * 10**9, transcendentals=0, bytes_accessed=8 * 10**6),
        name="tables",
    )(token_table, row_table, col_table, chan_table)
    packed, tables = lax.optimization_barrier((packed, tables))
    *splits, where_sum = tables
    tokens = splits[:3]

    with jax.named_scope("columns"):
        packed = jnp.concatenate([packed[:, :32, :].reshape(256, 128), packed[7, 32:, :]], axis=0)
        weights = exchange(jnp.broadcast_to(packed[None], (8, 264, 128)), COLUMN)

    block = POS_DEV // KEY_STEPS
    key_cat, value_cat = pl.pallas_call(
        keys_kernel,
        grid=(KEY_STEPS,),
        in_specs=[SMEM, whole(8, 128)] + [whole(VOCAB, D)] * 3 + [whole(384, D)] * 3 + [whole(D, 128)] * 2,
        out_specs=[middle(2, block, 384), middle(2, block, 256)],
        out_shape=[bf16(2, POS_DEV, 384), bf16(2, POS_DEV, 256)],
        compiler_params=params(),
        cost_estimate=pl.CostEstimate(flops=8 * 10**9, transcendentals=0, bytes_accessed=10**7),
        name="keys",
    )(index, token_ids.reshape(8, 128), *splits, w_key, w_value)

    size = LAT // LATENT_STEPS
    states = pl.pallas_call(
        attend_kernel,
        grid=(LATENT_STEPS,),
        in_specs=[SMEM, whole(8, 128), slab(size, D)]
        + [whole(VOCAB, D)] * 3
        + [whole(D, 128), whole(2, POS_DEV, 384), whole(2, POS_DEV, 256)],
        out_specs=slab(size // 8 * 9, 128),
        out_shape=shape(64 * 9, 128),
        scratch_shapes=[pltpu.VMEM((size, 128), jnp.float32)],
        compiler_params=params(),
        cost_estimate=pl.CostEstimate(flops=6 * 10**9, transcendentals=10**6, bytes_accessed=10**7),
        name="attend",
    )(index, weights[7, 256:264, :], where_sum, *tokens, w_query, key_cat, value_cat)

    with jax.named_scope("states"):
        states = exchange(states.reshape(64, 1, 1152), POS).reshape(64 * 9, 128)
    out_cat, in_cat, down_cat = pl.pallas_call(
        prepare_kernel,
        in_specs=[VMEM],
        out_specs=[VMEM] * 3,
        out_shape=[pltpu.VMEM((D, n), jnp.bfloat16) for n in (256, 128, 256)],
        compiler_params=params(),
        cost_estimate=pl.CostEstimate(flops=10**9, transcendentals=0, bytes_accessed=3 * 10**6),
        name="prepare",
    )(weights)
    partial_rows = pl.pallas_call(
        project_kernel,
        in_specs=[VMEM, VMEM],
        out_specs=VMEM,
        out_shape=shape(8, 64, 128),
        compiler_params=params(),
        name="project",
    )(near(states), near(out_cat))
    with jax.named_scope("projected"):
        projected = jnp.sum(exchange(partial_rows, HEAD), axis=0)
        rows = exchange(jnp.broadcast_to(projected[None], (8, 64, 128)), "z")
    outs = pl.pallas_call(
        latent_kernel,
        in_specs=[VMEM] * 3,
        out_specs=VMEM,
        out_shape=shape(512, 128),
        compiler_params=params(),
        name="latent",
    )(near(rows.reshape(512, 128)), near(in_cat), near(down_cat))
    with jax.named_scope("result"):
        own = jnp.sum(exchange(outs.reshape(8, 64, 128), "z"), axis=0)
        total = jnp.sum(exchange(jnp.broadcast_to(own[None], (8, 64, 128)), HEAD), axis=0)
        return (projected + total).reshape(8, D)


def solution(mesh):
    fine = Mesh(mesh.devices.reshape(8, 2, 4, 4, 2), ("z", "ylo", "x", "yhi", "core"))
    placed = (
        P(POS),
        P(),
        P(),
        P(),
        P(),
        P(None, HEAD),
        P(None, HEAD),
        P(None, HEAD),
        P(HEAD, POS),
        P(POS, HEAD),
        P(HEAD, POS),
    )
    return jax.shard_map(
        per_device, mesh=fine, in_specs=placed, out_specs=P(POS, None), check_vma=False
    )
```
